1024 devices in a mesh: seq: 64 (over z, core), chan: 16 (over y, x).
Axes of the slice: x: 4, y: 4, z: 32, core: 2. Of those that a mesh axis runs over, the one named last changes fastest.
Arguments:
- mixer_input: bfloat16 [8192, 2048], P('seq', 'chan'), may hold values from -6 to 6
- gate_branch: bfloat16 [8192, 2048], P('seq', 'chan'), may hold values from -6 to 6
- skip_gain: float32 [2048], P('chan'), may hold values from -3 to 3
- decay_rate: float32 [2048], P('chan'), may hold values from 0.1 to 512
- first_weight: float32 [33, 64], replicated, may hold values from -1 to 1
- first_bias: float32 [64], replicated, may hold values from -4 to 4
- second_weight: float32 [64, 64], replicated, may hold values from -0.75 to 0.75
- second_bias: float32 [64], replicated, may hold values from -4 to 4
- last_weight: float32 [64, 2048], P(None, 'chan'), may hold values from -0.75 to 0.75
- output_weight: bfloat16 [2048, 4096], P('chan'), may hold values from -0.1875 to 0.1875
Outputs:
- projected: bfloat16 [8192, 4096], P('seq', 'chan')
The draws below stay inside these ranges and needn't reach their ends.
All inputs are finite; a program needn't handle non-finite values.
Results may differ from the reference program's by a relative error of at most 0.0049.
Values may be sent and summed in bfloat16 or wider, within the bound.
A program may use at most 32 MiB of HBM per device.

```python
import math
import jax
import jax.numpy as jnp
from jax import lax

CHANNELS = 2048
D_MODEL = 4096
ORDER = 64
EMB = 33
SEQ = 8192


def draw_decay_rate(key, part):
    key_pick, key_slow, key_fast = jax.random.split(key, 3)
    keep_share = 0.5
    slow_rate = jax.random.uniform(key_slow, (CHANNELS,), jnp.float32, 0.1, 2.0)
    fast_rate = jnp.exp(jax.random.uniform(key_fast, (CHANNELS,), jnp.float32, math.log(2.0), math.log(SEQ / 16.0)))
    picked = jax.random.uniform(key_pick, (CHANNELS,), jnp.float32) < keep_share
    return jnp.where(picked, slow_rate, fast_rate)


def spiked(result, key, source, target, blocks, factor):
    owner, partner = [(jnp.arange(result.shape[dim]) // (result.shape[dim] // blocks)).reshape([-1 if axis == dim else 1 for axis in range(result.ndim)]) for dim in (source, target)]
    chosen = jax.random.permutation(key, blocks)[partner]
    strong = (owner == chosen) | (owner == (partner + blocks // 2) % blocks)
    return jnp.where(strong, factor * result, result)


def block_scale(rng, dims, shards, smallest, largest):
    gain = 1.0
    for position, shards_of in shards:
        heights = jax.random.uniform(jax.random.fold_in(jax.random.fold_in(rng, 6), position), (shards_of,), jnp.float32, smallest / len(shards), largest / len(shards))
        gain = gain * jnp.repeat(jnp.exp(heights), dims[position] // shards_of).reshape((-1,) + (1,) * (len(dims) - 1 - position))
    return gain


def centred(own_key, extent, scale, most, cuts=(), held_as=jnp.bfloat16):
    result = scale * jax.random.normal(own_key, extent, jnp.float32)
    if cuts:
        result = result * block_scale(own_key, extent, cuts, -0.22, 0.18)
    return jnp.clip(result, -most, most).astype(held_as)


def gaussian_with(rng, dims, width, limit, cuts, heavy, kind=jnp.bfloat16):
    drawn = width * jax.random.normal(rng, dims, jnp.float32)
    if cuts:
        drawn = drawn * block_scale(rng, dims, cuts, -0.22, 0.18)
    return jnp.clip(spiked(drawn, jax.random.fold_in(rng, 3), *heavy), -limit, limit).astype(kind)


def setup_inputs(seed: int = 0) -> dict:
    key_of = jax.random.split(jax.random.key(seed), 11)
    return {
        "mixer_input": centred(key_of[0], (SEQ, CHANNELS), 1.0, 6.0, ((0, 64), (1, 16))),
        "gate_branch": centred(key_of[1], (SEQ, CHANNELS), 1.0, 6.0, ((0, 64), (1, 16))),
        "skip_gain": centred(key_of[2], (CHANNELS,), 1.0, 3.0, ((0, 16),), jnp.float32),
        "decay_rate": draw_decay_rate(jax.random.fold_in(key_of[10], 71), 0),
        "first_weight": centred(key_of[4], (EMB, ORDER), EMB ** -0.5, 1.0, (), jnp.float32),
        "first_bias": centred(key_of[5], (ORDER,), 1.0, 4.0, (), jnp.float32),
        "second_weight": centred(key_of[6], (ORDER, ORDER), ORDER ** -0.5, 0.75, (), jnp.float32),
        "second_bias": centred(key_of[7], (ORDER,), 1.0, 4.0, (), jnp.float32),
        "last_weight": centred(key_of[8], (ORDER, CHANNELS), ORDER ** -0.5, 0.75, ((1, 16),), jnp.float32),
        "output_weight": gaussian_with(key_of[9], (CHANNELS, D_MODEL), CHANNELS ** -0.5, 0.1875, ((0, 16),), (0, 1, 16, 2.0)),
    }


def position_features(length, emb_width):
    band_count = (emb_width - 1) // 2
    positions = jnp.arange(length, dtype=jnp.int32)
    feature_rows = [positions.astype(jnp.float32) / length]
    for band_index in range(1, band_count + 1):
        frequency = min(length // 2, max(band_index, int((length / 2) ** ((band_index - 1) / (band_count - 1)))))
        phase_angle = (positions * frequency % length).astype(jnp.float32) * (2.0 * math.pi / length)
        feature_rows.append(jnp.cos(phase_angle))
        feature_rows.append(jnp.sin(phase_angle))
    return jnp.stack(feature_rows, axis=0)

def contract_first(left_matrix, right_matrix):
    return lax.dot_general(left_matrix, right_matrix, (((0,), (0,)), ((), ())), precision=lax.Precision.HIGHEST, preferred_element_type=jnp.float32)

def filter_taps(first_weight, first_bias, second_weight, second_bias, last_weight, decay_rate, length, emb_width):
    features = position_features(length, emb_width)
    hidden_one = jnp.sin(contract_first(first_weight, features) + first_bias[:, None])
    hidden_two = jnp.sin(contract_first(second_weight, hidden_one) + second_bias[:, None])
    shaped = contract_first(hidden_two, last_weight)
    positions = jnp.arange(length, dtype=jnp.int32).astype(jnp.float32)
    envelope = jnp.exp(-decay_rate[None, :] * (positions[:, None] / length))
    energy = jnp.expm1(-2.0 * decay_rate) / jnp.expm1(-2.0 * decay_rate / length)
    return shaped * envelope / jnp.sqrt(energy)[None, :]

def reference(mixer_input, gate_branch, skip_gain, decay_rate, first_weight, first_bias, second_weight, second_bias, last_weight, output_weight):
    kernel_taps = filter_taps(first_weight, first_bias, second_weight, second_bias, last_weight, decay_rate, SEQ, EMB)
    values = mixer_input.astype(jnp.float32)
    padded_length = 2 * SEQ
    spectrum = jnp.fft.rfft(values, n=padded_length, axis=0) * jnp.fft.rfft(kernel_taps, n=padded_length, axis=0)
    convolved = jnp.fft.irfft(spectrum, n=padded_length, axis=0)[:SEQ]
    gated_mix = (gate_branch.astype(jnp.float32) * (convolved + skip_gain[None, :] * values)).astype(jnp.bfloat16)
    return jnp.dot(gated_mix, output_weight, preferred_element_type=jnp.float32).astype(jnp.bfloat16)
```

```python
import functools
import math

import jax
import jax.numpy as jnp
import ml_dtypes
import numpy as np
from jax import lax
from jax.experimental import pallas as pl
from jax.experimental.pallas import tpu as pltpu
from jax.sharding import PartitionSpec as P

HIGHEST = lax.Precision.HIGHEST
F32 = jnp.float32
BF16 = jnp.bfloat16
MESH = pl.DeviceIdType.MESH


def band_frequencies(length, emb_width):
    band_count = (emb_width - 1) // 2
    return [
        min(length // 2, max(b, int((length / 2) ** ((b - 1) / (band_count - 1)))))
        for b in range(1, band_count + 1)
    ]


def two_terms(table):
    high = table.astype(np.float32).astype(ml_dtypes.bfloat16)
    low = (table - high.astype(np.float64)).astype(np.float32).astype(ml_dtypes.bfloat16)
    return high, low


def transform_tables(blocks, width):
    length = blocks * width
    k1 = np.arange(blocks)[:, None]
    b = np.arange(blocks)[None, :]
    across = 2.0 * math.pi * (k1 + 0.25) * b / blocks
    first = np.concatenate([np.cos(across), -np.sin(across)], axis=0)
    last = np.concatenate([np.cos(across).T, -np.sin(across).T], axis=1) / length
    j = np.arange(width)
    turn = 2.0 * math.pi * (k1 + 0.25) * j[None, :] / length
    twiddle = np.stack([np.cos(turn), np.sin(turn)]).astype(np.float32)
    within = 2.0 * math.pi * ((j[:, None] * j[None, :]) % width) / width
    cos, sin = np.cos(within), np.sin(within)
    middle = np.block([[cos, -sin], [sin, cos]])
    return (
        *two_terms(first),
        twiddle,
        *two_terms(middle),
        *two_terms(middle.T),
        *two_terms(last),
    )


def split(value):
    high = value.astype(BF16)
    return high, (value - high.astype(F32)).astype(BF16)


def dot(left, right):
    return jnp.dot(left, right, preferred_element_type=F32)


def dot_terms(left, right):
    (left_high, left_low), (right_high, right_low) = left, right
    return dot(left_high, right_high) + (dot(left_low, right_high) + dot(left_high, right_low))


def contract_first(left, right):
    return lax.dot_general(
        left, right, (((0,), (0,)), ((), ())), precision=HIGHEST, preferred_element_type=F32
    )


def taps_block(
    start, length, freqs, width, w1_ref, b1_ref, w2_ref, b2_ref, wl_ref, decay_ref, pad1, pad2, hid
):
    emb, order = w1_ref.shape
    rows = pad1.shape[0]
    row = lax.broadcasted_iota(jnp.int32, (rows, width), 0)
    time = start + lax.broadcasted_iota(jnp.int32, (rows, width), 1)
    freq = jnp.zeros((rows, width), jnp.int32)
    for band, f in enumerate(freqs):
        freq = jnp.where((row == 2 * band + 1) | (row == 2 * band + 2), f, freq)
    shift = jnp.where(lax.rem(row, 2) == 1, length // 4, 0)
    phase = lax.rem(time * freq + shift, length).astype(F32) * (2.0 * math.pi / length)
    features = jnp.where(row == 0, time.astype(F32) / length, jnp.sin(phase))
    features = jnp.where(row == emb, 1.0, jnp.where(row > emb, 0.0, features))
    pad1[...] = jnp.zeros_like(pad1)
    pad1[0:emb, :] = w1_ref[...]
    pad1[emb : emb + 1, :] = b1_ref[...]
    hid[0:order, :] = jnp.sin(contract_first(pad1[...], features))
    extra = lax.broadcasted_iota(jnp.int32, (hid.shape[0] - order, width), 0)
    hid[order:, :] = jnp.where(extra == 0, 1.0, 0.0)
    pad2[...] = jnp.zeros_like(pad2)
    pad2[0:order, :] = w2_ref[...]
    pad2[order : order + 1, :] = b2_ref[...]
    hidden_two = jnp.sin(contract_first(pad2[...], hid[...]))
    shaped = contract_first(wl_ref[...], hidden_two)
    chans = shaped.shape[0]
    rate = decay_ref[...]
    small = rate * (-2.0 / length)
    series = jnp.ones_like(small)
    for term in range(8, 1, -1):
        series = 1.0 + series * small * (1.0 / term)
    scale = lax.rsqrt((jnp.exp(-2.0 * rate) - 1.0) / (small * series))
    rates = jnp.broadcast_to(rate, (width, chans)).T
    scales = jnp.broadcast_to(scale, (width, chans)).T
    fraction = (start + lax.broadcasted_iota(jnp.int32, (chans, width), 1)).astype(F32) / length
    return shaped * jnp.exp(-rates * fraction) * scales


def convolve(per, recv, send, lhs, mid, first, twiddle, forward, backward, last):
    blocks, _, width = recv.shape
    both = 2 * per
    first_high, first_low = first
    source = jnp.concatenate([recv[:, i, :] for i in range(both)], axis=1)
    high, low = split(source)
    stage = dot(first_high, high) + (dot(first_low, high) + dot(first_high, low))
    cos, sin = twiddle[0], twiddle[1]
    for i in range(both):
        re = stage[:blocks, i * width : (i + 1) * width]
        im = stage[blocks:, i * width : (i + 1) * width]
        lhs[i * blocks : (i + 1) * blocks, :width] = re * cos + im * sin
        lhs[i * blocks : (i + 1) * blocks, width:] = im * cos - re * sin
    spectrum = dot_terms(split(lhs[...]), (forward[0][...], forward[1][...]))
    half = per * blocks
    x_re, x_im = spectrum[:half, :width], spectrum[:half, width:]
    h_re, h_im = spectrum[half:, :width], spectrum[half:, width:]
    lhs[:half, :width] = x_re * h_re - x_im * h_im
    lhs[:half, width:] = x_re * h_im + x_im * h_re
    stage = dot_terms(split(lhs[:half, :]), (backward[0][...], backward[1][...]))
    for i in range(per):
        re = stage[i * blocks : (i + 1) * blocks, :width]
        im = stage[i * blocks : (i + 1) * blocks, width:]
        mid[:blocks, i * width : (i + 1) * width] = re * cos - im * sin
        mid[blocks:, i * width : (i + 1) * width] = re * sin + im * cos
    result = dot_terms(last, split(mid[...]))
    for i in range(per):
        send[:, i, :] = result[:, i * width : (i + 1) * width]


def mixer_kernel(
    seq_size,
    chan_size,
    freqs,
    x_ref,
    gate_ref,
    skip_ref,
    decay_ref,
    w1_ref,
    b1_ref,
    w2_ref,
    b2_ref,
    wl_ref,
    first_high,
    first_low,
    twiddle,
    forward_high,
    forward_low,
    backward_high,
    backward_low,
    last_high,
    last_low,
    weight_hbm,
    out_ref,
    pad1,
    pad2,
    hid,
    send1,
    recv1,
    lhs,
    mid,
    send2,
    recv2,
    mixed,
    gathered,
    columns,
    send_sems,
    recv_sems,
    local_sem,
):
    block, chans = x_ref.shape
    per = chans // seq_size
    feats = out_ref.shape[1]
    d = lax.axis_index("seq")
    c = lax.axis_index("chan")

    def seq_peer(k):
        return lax.rem(d + k, seq_size)

    def chan_peer(k):
        return lax.rem(c + k, chan_size)

    barrier = pltpu.get_barrier_semaphore()

    @pl.loop(1, seq_size)
    def _(k):
        pl.semaphore_signal(
            barrier, inc=1, device_id={"seq": seq_peer(k)}, device_id_type=MESH
        )

    @pl.loop(1, chan_size)
    def _(k):
        pl.semaphore_signal(
            barrier, inc=1, device_id={"chan": chan_peer(k)}, device_id_type=MESH
        )

    own_columns = pltpu.make_async_copy(
        weight_hbm.at[:, pl.ds(pl.multiple_of(c * feats, feats), feats)],
        columns.at[pl.ds(pl.multiple_of(c * chans, chans), chans), :],
        local_sem,
    )
    own_columns.start()

    taps = taps_block(
        d * block,
        seq_size * block,
        freqs,
        block,
        w1_ref,
        b1_ref,
        w2_ref,
        b2_ref,
        wl_ref,
        decay_ref,
        pad1,
        pad2,
        hid,
    )
    turned = x_ref[...].astype(F32).T
    for i in range(per):
        send1[:, i, :] = turned[i * seq_size : (i + 1) * seq_size, :]
        send1[:, per + i, :] = taps[i * seq_size : (i + 1) * seq_size, :]

    pl.semaphore_wait(barrier, seq_size - 1 + chan_size - 1)

    @pl.loop(1, seq_size)
    def _(k):
        p = seq_peer(k)
        pltpu.make_async_remote_copy(
            src_ref=send1.at[p],
            dst_ref=recv1.at[d],
            send_sem=send_sems.at[0],
            recv_sem=recv_sems.at[0],
            device_id={"seq": p},
            device_id_type=MESH,
        ).start()

    @pl.loop(1, chan_size)
    def _(k):
        p = chan_peer(k)
        pltpu.make_async_remote_copy(
            src_ref=weight_hbm.at[:, pl.ds(pl.multiple_of(p * feats, feats), feats)],
            dst_ref=columns.at[pl.ds(pl.multiple_of(c * chans, chans), chans), :],
            send_sem=send_sems.at[1],
            recv_sem=recv_sems.at[1],
            device_id={"chan": p},
            device_id_type=MESH,
        ).start()

    recv1[d] = send1[d]

    def wait_bytes(ref, sem):
        pltpu.make_async_copy(ref, ref, sem).wait()

    others = pl.ds(0, seq_size - 1)
    wait_bytes(recv1.at[others], recv_sems.at[0])

    convolve(
        per,
        recv1,
        send2,
        lhs,
        mid,
        (first_high[...], first_low[...]),
        twiddle,
        (forward_high, forward_low),
        (backward_high, backward_low),
        (last_high[...], last_low[...]),
    )

    @pl.loop(1, seq_size)
    def _(k):
        p = seq_peer(k)
        pltpu.make_async_remote_copy(
            src_ref=send2.at[p],
            dst_ref=recv2.at[d],
            send_sem=send_sems.at[2],
            recv_sem=recv_sems.at[2],
            device_id={"seq": p},
            device_id_type=MESH,
        ).start()

    recv2[d] = send2[d]
    skipped = skip_ref[...] * x_ref[...].astype(F32)
    gate = gate_ref[...].astype(F32)
    wait_bytes(recv2.at[others], recv_sems.at[2])
    convolved = jnp.concatenate([recv2[:, i, :] for i in range(per)], axis=0).T
    mixed[...] = (gate * (convolved + skipped)).astype(BF16)

    here = gathered.at[:, pl.ds(pl.multiple_of(c * chans, chans), chans)]

    @pl.loop(1, chan_size)
    def _(k):
        pltpu.make_async_remote_copy(
            src_ref=mixed,
            dst_ref=here,
            send_sem=send_sems.at[3],
            recv_sem=recv_sems.at[3],
            device_id={"chan": chan_peer(k)},
            device_id_type=MESH,
        ).start()

    here[...] = mixed[...]
    own_columns.wait()
    rest = pl.ds(0, (chan_size - 1) * chans)
    wait_bytes(columns.at[rest, :], recv_sems.at[1])
    wait_bytes(gathered.at[:, rest], recv_sems.at[3])
    out_ref[...] = dot(gathered[...], columns[...]).astype(out_ref.dtype)

    wait_bytes(send1.at[others], send_sems.at[0])
    wait_bytes(columns.at[rest, :], send_sems.at[1])
    wait_bytes(send2.at[others], send_sems.at[2])
    wait_bytes(gathered.at[:, rest], send_sems.at[3])


def shards(
    mixer_input,
    gate_branch,
    skip_gain,
    decay_rate,
    first_weight,
    first_bias,
    second_weight,
    second_bias,
    last_weight,
    output_weight,
):
    block, chans = mixer_input.shape
    seq_size = lax.axis_size("seq")
    chan_size = lax.axis_size("chan")
    emb, order = first_weight.shape
    feats = output_weight.shape[1] // chan_size
    per = chans // seq_size
    length = block * seq_size
    tables = transform_tables(seq_size, block)
    vmem = pl.BlockSpec(memory_space=pltpu.VMEM)
    return pl.pallas_call(
        functools.partial(mixer_kernel, seq_size, chan_size, band_frequencies(length, emb)),
        out_shape=jax.ShapeDtypeStruct((block, feats), BF16),
        in_specs=[vmem] * (9 + len(tables)) + [pl.BlockSpec(memory_space=pl.ANY)],
        out_specs=vmem,
        scratch_shapes=[
            pltpu.VMEM((-(-(emb + 1) // 8) * 8, order), F32),
            pltpu.VMEM((order + 8, order), F32),
            pltpu.VMEM((order + 8, block), F32),
            pltpu.VMEM((seq_size, 2 * per, block), F32),
            pltpu.VMEM((seq_size, 2 * per, block), F32),
            pltpu.VMEM((2 * chans, 2 * block), F32),
            pltpu.VMEM((2 * seq_size, per * block), F32),
            pltpu.VMEM((seq_size, per, block), F32),
            pltpu.VMEM((seq_size, per, block), F32),
            pltpu.VMEM((block, chans), BF16),
            pltpu.VMEM((block, chan_size * chans), BF16),
            pltpu.VMEM((chan_size * chans, feats), BF16),
            pltpu.SemaphoreType.DMA((4,)),
            pltpu.SemaphoreType.DMA((4,)),
            pltpu.SemaphoreType.DMA,
        ],
        compiler_params=pltpu.CompilerParams(
            collective_id=0, has_side_effects=True, vmem_limit_bytes=32 << 20
        ),
    )(
        mixer_input,
        gate_branch,
        skip_gain.reshape(1, chans),
        decay_rate.reshape(1, chans),
        first_weight,
        first_bias.reshape(1, order),
        second_weight,
        second_bias.reshape(1, order),
        last_weight,
        *[jnp.asarray(table) for table in tables],
        output_weight,
    )


def solution(mesh):
    in_specs = (
        P("seq", "chan"),
        P("seq", "chan"),
        P("chan"),
        P("chan"),
        P(),
        P(),
        P(),
        P(),
        P(None, "chan"),
        P("chan", None),
    )
    out_specs = P("seq", "chan")
    return jax.shard_map(shards, mesh=mesh, in_specs=in_specs, out_specs=out_specs, check_vma=False)
```

```python
import functools
import math

import jax
import jax.numpy as jnp
import ml_dtypes
import numpy as np
from jax import lax
from jax.experimental import pallas as pl
from jax.experimental.pallas import tpu as pltpu
from jax.sharding import PartitionSpec as P

HIGHEST = lax.Precision.HIGHEST
F32 = jnp.float32
BF16 = jnp.bfloat16
MESH = pl.DeviceIdType.MESH


def band_frequencies(length, emb_width):
    band_count = (emb_width - 1) // 2
    return [
        min(length // 2, max(b, int((length / 2) ** ((b - 1) / (band_count - 1)))))
        for b in range(1, band_count + 1)
    ]


def two_terms(table):
    high = table.astype(np.float32).astype(ml_dtypes.bfloat16)
    low = (table - high.astype(np.float64)).astype(np.float32).astype(ml_dtypes.bfloat16)
    return high, low


def transform_tables(blocks, width):
    length = blocks * width
    k1 = np.arange(blocks)[:, None]
    b = np.arange(blocks)[None, :]
    across = 2.0 * math.pi * (k1 + 0.25) * b / blocks
    first = np.concatenate([np.cos(across), -np.sin(across)], axis=0)
    last = np.concatenate([np.cos(across).T, -np.sin(across).T], axis=1) / length
    j = np.arange(width)
    turn = 2.0 * math.pi * (k1 + 0.25) * j[None, :] / length
    twiddle = np.concatenate([np.cos(turn), np.sin(turn)]).astype(np.float32)
    within = 2.0 * math.pi * ((j[:, None] * j[None, :]) % width) / width
    cos, sin = np.cos(within), np.sin(within)
    middle = np.concatenate(two_terms(np.block([[cos, -sin], [sin, cos]])), axis=0)
    first_high, first_low = two_terms(first)
    first = np.concatenate([first_high, first_low, first_high, first_low], axis=1)
    last = np.concatenate(two_terms(last), axis=1)
    return twiddle, middle, first, last


def split(value):
    high = value.astype(BF16)
    return high, (value - high.astype(F32)).astype(BF16)


def dot(left, right):
    return jnp.dot(left, right, preferred_element_type=F32)


def dot_nt(left, right):
    return lax.dot_general(left, right, (((1,), (1,)), ((), ())), preferred_element_type=F32)


def contract_first(left, right):
    return lax.dot_general(
        left, right, (((0,), (0,)), ((), ())), precision=HIGHEST, preferred_element_type=F32
    )


def taps_block(
    start, length, freqs, width, w1_ref, b1_ref, w2_ref, b2_ref, wl_ref, decay_ref, pad1, pad2, hid
):
    emb, order = w1_ref.shape
    rows = pad1.shape[0]
    row = lax.broadcasted_iota(jnp.int32, (rows, width), 0)
    time = start + lax.broadcasted_iota(jnp.int32, (rows, width), 1)
    freq = jnp.zeros((rows, width), jnp.int32)
    for band, f in enumerate(freqs):
        freq = jnp.where((row == 2 * band + 1) | (row == 2 * band + 2), f, freq)
    shift = jnp.where(lax.rem(row, 2) == 1, length // 4, 0)
    phase = lax.rem(time * freq + shift, length).astype(F32) * (2.0 * math.pi / length)
    features = jnp.where(row == 0, time.astype(F32) / length, jnp.sin(phase))
    features = jnp.where(row == emb, 1.0, jnp.where(row > emb, 0.0, features))
    pad1[...] = jnp.zeros_like(pad1)
    pad1[0:emb, :] = w1_ref[...]
    pad1[emb : emb + 1, :] = b1_ref[...]
    hid[0:order, :] = jnp.sin(contract_first(pad1[...], features))
    extra = lax.broadcasted_iota(jnp.int32, (hid.shape[0] - order, width), 0)
    hid[order:, :] = jnp.where(extra == 0, 1.0, 0.0)
    pad2[...] = jnp.zeros_like(pad2)
    pad2[0:order, :] = w2_ref[...]
    pad2[order : order + 1, :] = b2_ref[...]
    hidden_two = jnp.sin(contract_first(pad2[...], hid[...]))
    shaped = contract_first(wl_ref[...], hidden_two)
    chans = shaped.shape[0]
    rate = decay_ref[...]
    small = rate * (-2.0 / length)
    series = jnp.ones_like(small)
    for term in range(8, 1, -1):
        series = 1.0 + series * small * (1.0 / term)
    scale = lax.rsqrt((jnp.exp(-2.0 * rate) - 1.0) / (small * series))
    rates = jnp.broadcast_to(rate, (width, chans)).T
    scales = jnp.broadcast_to(scale, (width, chans)).T
    fraction = (start + lax.broadcasted_iota(jnp.int32, (chans, width), 1)).astype(F32) / length
    return shaped * jnp.exp(-rates * fraction) * scales


def convolve(per, recv, send, lhs, mid, twiddle, middle, first, last):
    blocks, _, width = recv.shape
    both = 2 * per
    high, low = split(jnp.concatenate([recv[:, i, :] for i in range(both)], axis=1))
    stage = dot(first[...], jnp.concatenate([high, high, low, low], axis=0))
    cos, sin = twiddle[:blocks, :], twiddle[blocks:, :]
    for i in range(both):
        re = stage[:blocks, i * width : (i + 1) * width]
        im = stage[blocks:, i * width : (i + 1) * width]
        lhs[i * blocks : (i + 1) * blocks, :width] = re * cos + im * sin
        lhs[i * blocks : (i + 1) * blocks, width:] = im * cos - re * sin
    table_high, table_low = middle[: 2 * width, :], middle[2 * width :, :]
    high, low = split(lhs[...])
    spectrum = dot(high, table_high) + (dot(low, table_high) + dot(high, table_low))
    half = per * blocks
    x_re, x_im = spectrum[:half, :width], spectrum[:half, width:]
    h_re, h_im = spectrum[half:, :width], spectrum[half:, width:]
    product = jnp.concatenate([x_re * h_re - x_im * h_im, x_re * h_im + x_im * h_re], axis=1)
    high, low = split(product)
    stage = dot_nt(high, table_high) + (dot_nt(low, table_high) + dot_nt(high, table_low))
    for i in range(per):
        re = stage[i * blocks : (i + 1) * blocks, :width]
        im = stage[i * blocks : (i + 1) * blocks, width:]
        mid[:blocks, i * width : (i + 1) * width] = re * cos - im * sin
        mid[blocks:, i * width : (i + 1) * width] = re * sin + im * cos
    high, low = split(mid[...])
    table = last[...]
    result = dot(table, jnp.concatenate([high, high], axis=0))
    result += dot(table, jnp.concatenate([low, low], axis=0))
    for i in range(per):
        send[:, i, :] = result[:, i * width : (i + 1) * width]


def mixer_kernel(seq_size, chan_size, freqs, arrays, *refs):
    sources, weight_hbm, out_ref = refs[:arrays], refs[arrays], refs[arrays + 1]
    held = refs[arrays + 2 : 2 * arrays + 2]
    x_ref, gate_ref, skip_ref, decay_ref, w1_ref, b1_ref, w2_ref, b2_ref, wl_ref = held[:9]
    (
        pad1,
        pad2,
        hid,
        send1,
        recv1,
        lhs,
        mid,
        send2,
        recv2,
        mixed,
        gathered,
        columns,
        send_sems,
        recv_sems,
        local_sems,
    ) = refs[2 * arrays + 2 :]
    block, chans = x_ref.shape
    per = chans // seq_size
    feats = out_ref.shape[1]
    d = lax.axis_index("seq")
    c = lax.axis_index("chan")

    def seq_peer(k):
        return lax.rem(d + k, seq_size)

    def chan_peer(k):
        return lax.rem(c + k, chan_size)

    loads = [
        pltpu.make_async_copy(source, target, local_sems.at[i])
        for i, (source, target) in enumerate(zip(sources, held))
    ]
    for load in loads:
        load.start()
    barrier = pltpu.get_barrier_semaphore()

    @pl.loop(1, seq_size)
    def _(k):
        pl.semaphore_signal(
            barrier, inc=1, device_id={"seq": seq_peer(k)}, device_id_type=MESH
        )

    @pl.loop(1, chan_size)
    def _(k):
        pl.semaphore_signal(
            barrier, inc=1, device_id={"chan": chan_peer(k)}, device_id_type=MESH
        )

    own_columns = pltpu.make_async_copy(
        weight_hbm.at[:, pl.ds(pl.multiple_of(c * feats, feats), feats)],
        columns.at[pl.ds(pl.multiple_of(c * chans, chans), chans), :],
        local_sems.at[arrays],
    )
    own_columns.start()
    for load in loads:
        load.wait()

    taps = taps_block(
        d * block,
        seq_size * block,
        freqs,
        block,
        w1_ref,
        b1_ref,
        w2_ref,
        b2_ref,
        wl_ref,
        decay_ref,
        pad1,
        pad2,
        hid,
    )
    turned = x_ref[...].astype(F32).T
    for i in range(per):
        send1[:, i, :] = turned[i * seq_size : (i + 1) * seq_size, :]
        send1[:, per + i, :] = taps[i * seq_size : (i + 1) * seq_size, :]

    pl.semaphore_wait(barrier, seq_size - 1 + chan_size - 1)

    def wait_bytes(ref, sem):
        pltpu.make_async_copy(ref, ref, sem).wait()

    others = pl.ds(0, seq_size - 1)
    rest = pl.ds(0, (chan_size - 1) * chans)

    @pl.loop(1, seq_size)
    def _(k):
        p = seq_peer(k)
        pltpu.make_async_remote_copy(
            src_ref=send1.at[p],
            dst_ref=recv1.at[d],
            send_sem=send_sems.at[0],
            recv_sem=recv_sems.at[0],
            device_id={"seq": p},
            device_id_type=MESH,
        ).start()


    @pl.loop(1, chan_size)
    def _(k):
        p = chan_peer(k)
        pltpu.make_async_remote_copy(
            src_ref=weight_hbm.at[:, pl.ds(pl.multiple_of(p * feats, feats), feats)],
            dst_ref=columns.at[pl.ds(pl.multiple_of(c * chans, chans), chans), :],
            send_sem=send_sems.at[1],
            recv_sem=recv_sems.at[1],
            device_id={"chan": p},
            device_id_type=MESH,
        ).start()

    recv1[d] = send1[d]

    wait_bytes(recv1.at[others], recv_sems.at[0])

    convolve(per, recv1, send2, lhs, mid, *held[9:])


    @pl.loop(1, seq_size)
    def _(k):
        p = seq_peer(k)
        pltpu.make_async_remote_copy(
            src_ref=send2.at[p],
            dst_ref=recv2.at[d],
            send_sem=send_sems.at[2],
            recv_sem=recv_sems.at[2],
            device_id={"seq": p},
            device_id_type=MESH,
        ).start()

    recv2[d] = send2[d]
    skipped = skip_ref[...] * x_ref[...].astype(F32)
    gate = gate_ref[...].astype(F32)
    wait_bytes(recv2.at[others], recv_sems.at[2])
    convolved = jnp.concatenate([recv2[:, i, :] for i in range(per)], axis=0).T
    mixed[...] = (gate * (convolved + skipped)).astype(BF16)

    here = gathered.at[:, pl.ds(pl.multiple_of(c * chans, chans), chans)]

    @pl.loop(1, chan_size)
    def _(k):
        pltpu.make_async_remote_copy(
            src_ref=mixed,
            dst_ref=here,
            send_sem=send_sems.at[3],
            recv_sem=recv_sems.at[3],
            device_id={"chan": chan_peer(k)},
            device_id_type=MESH,
        ).start()

    here[...] = mixed[...]
    own_columns.wait()
    wait_bytes(columns.at[rest, :], recv_sems.at[1])
    wait_bytes(gathered.at[:, rest], recv_sems.at[3])
    out_ref[...] = dot(gathered[...], columns[...]).astype(out_ref.dtype)

    wait_bytes(send1.at[others], send_sems.at[0])
    wait_bytes(columns.at[rest, :], send_sems.at[1])
    wait_bytes(send2.at[others], send_sems.at[2])
    wait_bytes(gathered.at[:, rest], send_sems.at[3])


def shards(
    mixer_input,
    gate_branch,
    skip_gain,
    decay_rate,
    first_weight,
    first_bias,
    second_weight,
    second_bias,
    last_weight,
    output_weight,
):
    block, chans = mixer_input.shape
    seq_size = lax.axis_size("seq")
    chan_size = lax.axis_size("chan")
    emb, order = first_weight.shape
    feats = output_weight.shape[1] // chan_size
    per = chans // seq_size
    length = block * seq_size
    held = [
        mixer_input,
        gate_branch,
        skip_gain.reshape(1, chans),
        decay_rate.reshape(1, chans),
        first_weight,
        first_bias.reshape(1, order),
        second_weight,
        second_bias.reshape(1, order),
        last_weight,
        *[jnp.asarray(table) for table in transform_tables(seq_size, block)],
    ]
    return pl.pallas_call(
        functools.partial(
            mixer_kernel, seq_size, chan_size, band_frequencies(length, emb), len(held)
        ),
        out_shape=jax.ShapeDtypeStruct((block, feats), BF16),
        in_specs=[pl.BlockSpec(memory_space=pltpu.HBM)] * (len(held) + 1),
        out_specs=pl.BlockSpec(memory_space=pltpu.VMEM),
        scratch_shapes=[
            *[pltpu.VMEM(value.shape, value.dtype) for value in held],
            pltpu.VMEM((-(-(emb + 1) // 8) * 8, order), F32),
            pltpu.VMEM((order + 8, order), F32),
            pltpu.VMEM((order + 8, block), F32),
            pltpu.VMEM((seq_size, 2 * per, block), F32),
            pltpu.VMEM((seq_size, 2 * per, block), F32),
            pltpu.VMEM((2 * chans, 2 * block), F32),
            pltpu.VMEM((2 * seq_size, per * block), F32),
            pltpu.VMEM((seq_size, per, block), F32),
            pltpu.VMEM((seq_size, per, block), F32),
            pltpu.VMEM((block, chans), BF16),
            pltpu.VMEM((block, chan_size * chans), BF16),
            pltpu.VMEM((chan_size * chans, feats), BF16),
            pltpu.SemaphoreType.DMA((4,)),
            pltpu.SemaphoreType.DMA((4,)),
            pltpu.SemaphoreType.DMA((len(held) + 1,)),
        ],
        compiler_params=pltpu.CompilerParams(
            collective_id=0, has_side_effects=True, vmem_limit_bytes=62 << 20
        ),
    )(*held, output_weight)


def solution(mesh):
    in_specs = (
        P("seq", "chan"),
        P("seq", "chan"),
        P("chan"),
        P("chan"),
        P(),
        P(),
        P(),
        P(),
        P(None, "chan"),
        P("chan", None),
    )
    out_specs = P("seq", "chan")
    return jax.shard_map(shards, mesh=mesh, in_specs=in_specs, out_specs=out_specs, check_vma=False)
```

```python
import functools
import math

import jax
import jax.numpy as jnp
import ml_dtypes
import numpy as np
from jax import lax
from jax.experimental import pallas as pl
from jax.experimental.pallas import tpu as pltpu
from jax.sharding import PartitionSpec as P

HIGHEST = lax.Precision.HIGHEST
F32 = jnp.float32
BF16 = jnp.bfloat16
MESH = pl.DeviceIdType.MESH


def band_frequencies(length, emb_width):
    band_count = (emb_width - 1) // 2
    return [
        min(length // 2, max(b, int((length / 2) ** ((b - 1) / (band_count - 1)))))
        for b in range(1, band_count + 1)
    ]


def two_terms(table):
    high = table.astype(np.float32).astype(ml_dtypes.bfloat16)
    low = (table - high.astype(np.float64)).astype(np.float32).astype(ml_dtypes.bfloat16)
    return high, low


def transform_tables(blocks, width):
    length = blocks * width
    k1 = np.arange(blocks)[:, None]
    b = np.arange(blocks)[None, :]
    across = 2.0 * math.pi * (k1 + 0.25) * b / blocks
    first = np.concatenate([np.cos(across), -np.sin(across)], axis=0)
    last = np.concatenate([np.cos(across).T, -np.sin(across).T], axis=1) / length
    j = np.arange(width)
    turn = 2.0 * math.pi * (k1 + 0.25) * j[None, :] / length
    twiddle = np.concatenate([np.cos(turn), np.sin(turn)]).astype(np.float32)
    within = 2.0 * math.pi * ((j[:, None] * j[None, :]) % width) / width
    cos, sin = np.cos(within), np.sin(within)
    middle = np.concatenate(two_terms(np.block([[cos, -sin], [sin, cos]])), axis=0)
    first = np.stack(
        [np.concatenate(two_terms(half) * 2, axis=1) for half in np.split(first, 2, axis=1)]
    )
    last = np.concatenate(two_terms(last), axis=1)
    return twiddle, middle, first, last


def split(value):
    high = value.astype(BF16)
    return high, (value - high.astype(F32)).astype(BF16)


def dot(left, right):
    return jnp.dot(left, right, preferred_element_type=F32)


def dot_nt(left, right):
    return lax.dot_general(left, right, (((1,), (1,)), ((), ())), preferred_element_type=F32)


def contract_first(left, right):
    return lax.dot_general(
        left, right, (((0,), (0,)), ((), ())), precision=HIGHEST, preferred_element_type=F32
    )


def hidden_block(start, length, freqs, width, w1_ref, b1_ref, w2_ref, b2_ref, pad1, pad2, hid, out):
    emb, order = w1_ref.shape
    rows = pad1.shape[0]
    row = lax.broadcasted_iota(jnp.int32, (rows, width), 0)
    time = start + lax.broadcasted_iota(jnp.int32, (rows, width), 1)
    freq = jnp.zeros((rows, width), jnp.int32)
    for band, f in enumerate(freqs):
        freq = jnp.where((row == 2 * band + 1) | (row == 2 * band + 2), f, freq)
    shift = jnp.where(lax.rem(row, 2) == 1, length // 4, 0)
    phase = lax.rem(time * freq + shift, length).astype(F32) * (2.0 * math.pi / length)
    features = jnp.where(row == 0, time.astype(F32) / length, jnp.sin(phase))
    features = jnp.where(row == emb, 1.0, jnp.where(row > emb, 0.0, features))
    pad1[...] = jnp.zeros_like(pad1)
    pad1[0:emb, :] = w1_ref[...]
    pad1[emb : emb + 1, :] = b1_ref[...]
    hid[0:order, :] = jnp.sin(contract_first(pad1[...], features))
    extra = lax.broadcasted_iota(jnp.int32, (hid.shape[0] - order, width), 0)
    hid[order:, :] = jnp.where(extra == 0, 1.0, 0.0)
    pad2[...] = jnp.zeros_like(pad2)
    pad2[0:order, :] = w2_ref[...]
    pad2[order : order + 1, :] = b2_ref[...]
    out[...] = jnp.sin(contract_first(pad2[...], hid[...]))


def filter_taps(start, length, order, params, hidden):
    rate = params[:, order : order + 1]
    shaped = jnp.dot(params[:, :order], hidden, precision=HIGHEST, preferred_element_type=F32)
    small = rate * (-2.0 / length)
    series = jnp.ones_like(small)
    for term in range(8, 1, -1):
        series = 1.0 + series * small * (1.0 / term)
    scale = lax.rsqrt((jnp.exp(-2.0 * rate) - 1.0) / (small * series))
    fraction = (start + lax.broadcasted_iota(jnp.int32, shaped.shape, 1)).astype(F32) / length
    return shaped * jnp.exp(-rate * fraction) * scale


def spectrum(blocks, halves, lhs, twiddle, middle, first):
    width = twiddle.shape[1]
    stage = None
    for which, ref in halves:
        per = ref.shape[1]
        high, low = split(jnp.concatenate([ref[:, i, :] for i in range(per)], axis=1))
        part = dot(first[which], jnp.concatenate([high, high, low, low], axis=0))
        stage = part if stage is None else stage + part
    cos, sin = twiddle[:blocks, :], twiddle[blocks:, :]
    for i in range(per):
        re = stage[:blocks, i * width : (i + 1) * width]
        im = stage[blocks:, i * width : (i + 1) * width]
        lhs[i * blocks : (i + 1) * blocks, :width] = re * cos + im * sin
        lhs[i * blocks : (i + 1) * blocks, width:] = im * cos - re * sin
    table_high, table_low = middle[: 2 * width, :], middle[2 * width :, :]
    high, low = split(lhs[...])
    return dot(high, table_high) + (dot(low, table_high) + dot(high, table_low))


def multiply(left, right):
    width = left.shape[1] // 2
    left_re, left_im, right_re, right_im = left[:, :width], left[:, width:], right[:, :width], right[:, width:]
    return jnp.concatenate(
        [left_re * right_re - left_im * right_im, left_re * right_im + left_im * right_re], axis=1
    )


def inverse(blocks, product, which, mid, twiddle, middle, last, out):
    width = twiddle.shape[1]
    table_high, table_low = middle[: 2 * width, :], middle[2 * width :, :]
    high, low = split(product)
    stage = dot_nt(high, table_high) + (dot_nt(low, table_high) + dot_nt(high, table_low))
    cos, sin = twiddle[:blocks, :], twiddle[blocks:, :]
    per = out.shape[1]
    for i in range(per):
        re = stage[i * blocks : (i + 1) * blocks, :width]
        im = stage[i * blocks : (i + 1) * blocks, width:]
        mid[:blocks, i * width : (i + 1) * width] = re * cos - im * sin
        mid[blocks:, i * width : (i + 1) * width] = re * sin + im * cos
    high, low = split(mid[...])
    table = last[which * (blocks // 2) : (which + 1) * (blocks // 2), :]
    result = dot(table, jnp.concatenate([high, high], axis=0))
    result += dot(table, jnp.concatenate([low, low], axis=0))
    for i in range(per):
        out[:, i, :] = result[:, i * width : (i + 1) * width]


def mixer_kernel(seq_size, chan_size, owners, freqs, arrays, *refs):
    sources, weight_hbm, out_ref = refs[:arrays], refs[arrays], refs[arrays + 1]
    held = refs[arrays + 2 : 2 * arrays + 2]
    x_ref, gate_ref, skip_ref, decay_ref, w1_ref, b1_ref, w2_ref, b2_ref, wl_ref = held[:9]
    twiddle, middle, first, last = held[9:]
    (
        pad1,
        pad2,
        hid,
        hidden,
        rows,
        params,
        all_params,
        send_taps,
        recv_taps,
        send_x,
        recv_x,
        lhs,
        taps_spectrum,
        product,
        mid,
        send_y,
        recv_y,
        mixed,
        gathered,
        columns,
        send_sems,
        recv_sems,
        local_sems,
    ) = refs[2 * arrays + 2 :]
    block, chans = x_ref.shape
    order = w1_ref.shape[1]
    length = seq_size * block
    half = seq_size // 2
    per = chans // owners
    share = seq_size // chan_size
    feats = out_ref.shape[1]
    d = lax.axis_index("seq")
    c = lax.axis_index("chan")
    is_owner = d < owners

    def chan_peer(k):
        return lax.rem(c + k, chan_size)

    def wait_bytes(ref, sem):
        pltpu.make_async_copy(ref, ref, sem).wait()

    def to_seq(source, target, lane, landing, p):
        pltpu.make_async_remote_copy(
            src_ref=source,
            dst_ref=target,
            send_sem=send_sems.at[lane],
            recv_sem=recv_sems.at[landing],
            device_id={"seq": p},
            device_id_type=MESH,
        ).start()

    def to_chan(source, target, lane, p):
        pltpu.make_async_remote_copy(
            src_ref=source,
            dst_ref=target,
            send_sem=send_sems.at[lane],
            recv_sem=recv_sems.at[lane],
            device_id={"chan": p},
            device_id_type=MESH,
        ).start()

    loads = [
        pltpu.make_async_copy(source, target, local_sems.at[i])
        for i, (source, target) in enumerate(zip(sources, held))
    ]
    for load in loads:
        load.start()
    barrier = pltpu.get_barrier_semaphore()

    @pl.when(is_owner)
    def _():
        @pl.loop(1, seq_size)
        def _(k):
            p = lax.rem(d + k, seq_size)
            pl.semaphore_signal(barrier, inc=1, device_id={"seq": p}, device_id_type=MESH)

    @pl.loop(1, chan_size)
    def _(k):
        pl.semaphore_signal(
            barrier, inc=1, device_id={"chan": chan_peer(k)}, device_id_type=MESH
        )

    own_columns = pltpu.make_async_copy(
        weight_hbm.at[:, pl.ds(pl.multiple_of(c * feats, feats), feats)],
        columns.at[pl.ds(pl.multiple_of(c * chans, chans), chans), :],
        local_sems.at[arrays],
    )
    own_columns.start()
    for load in loads:
        load.wait()

    send_x[...] = x_ref[...].astype(F32).T.reshape(owners, per, block)

    @pl.when(is_owner)
    def _():
        rows[...] = jnp.zeros_like(rows)
        rows[:order, :] = wl_ref[...]
        rows[order : order + 1, :] = decay_ref[...]
        params[...] = rows[...].T.reshape(owners, per, block)
        pl.semaphore_wait(barrier, owners - 1 + chan_size - 1)

    @pl.when(jnp.logical_not(is_owner))
    def _():
        pl.semaphore_wait(barrier, owners + chan_size - 1)

    @pl.loop(0, owners)
    def _(o):
        @pl.when(o != d)
        def _():
            to_seq(send_x.at[o], recv_x.at[d], 0, jnp.where(d < half, 0, 1), o)

    others = pl.ds(0, (chan_size - 1))

    @pl.when(is_owner)
    def _():
        @pl.loop(1, chan_size)
        def _(k):
            to_chan(params.at[d], all_params.at[c], 2, chan_peer(k))

        all_params[c] = params[d]
        recv_x[d] = send_x[d]
        start = c * (share * block)
        hidden_block(
            start,
            length,
            freqs,
            share * block,
            w1_ref,
            b1_ref,
            w2_ref,
            b2_ref,
            pad1,
            pad2,
            hid,
            hidden,
        )
        wait_bytes(all_params.at[others], recv_sems.at[2])
        taps = filter_taps(
            start, length, order, all_params[...].reshape(chan_size * per, block), hidden[...]
        )
        for q in range(share):
            send_taps[:, q] = taps[:, q * block : (q + 1) * block].reshape(chan_size, per, block)
        here = pl.ds(c * share, share)

        @pl.loop(1, chan_size)
        def _(k):
            p = chan_peer(k)
            to_chan(send_taps.at[p], recv_taps.at[here], 3, p)

        recv_taps[here] = send_taps[c]

    @pl.loop(1, chan_size)
    def _(k):
        p = chan_peer(k)
        to_chan(
            weight_hbm.at[:, pl.ds(pl.multiple_of(p * feats, feats), feats)],
            columns.at[pl.ds(pl.multiple_of(c * chans, chans), chans), :],
            4,
            p,
        )

    early, late = pl.ds(0, half), pl.ds(half, half)

    @pl.when(is_owner)
    def _():
        wait_bytes(recv_taps.at[pl.ds(0, (chan_size - 1) * share)], recv_sems.at[3])
        taps_spectrum[...] = spectrum(
            seq_size,
            [(0, recv_taps.at[early]), (1, recv_taps.at[late])],
            lhs,
            twiddle,
            middle,
            first,
        )
        wait_bytes(recv_x.at[pl.ds(0, half - 1)], recv_sems.at[0])
        inputs = spectrum(seq_size, [(0, recv_x.at[early])], lhs, twiddle, middle, first)
        product[...] = multiply(inputs, taps_spectrum[...])
        inverse(
            seq_size, product[...], 0, mid, twiddle, middle, last, send_y.at[early]
        )

        @pl.loop(1, half)
        def _(k):
            p = lax.rem(d + k, half)
            to_seq(send_y.at[p], recv_y.at[d], 1, 5, p)

        recv_y[d] = send_y[d]
        wait_bytes(recv_y.at[pl.ds(0, owners - 1)], recv_sems.at[5])

    @pl.when(jnp.logical_not(is_owner))
    def _():
        wait_bytes(recv_y, recv_sems.at[5])

    convolved = recv_y[...].reshape(chans, block).T
    skipped = skip_ref[...] * x_ref[...].astype(F32)
    mixed[...] = (gate_ref[...].astype(F32) * (convolved + skipped)).astype(BF16)
    place = gathered.at[:, pl.ds(pl.multiple_of(c * chans, chans), chans)]

    @pl.loop(1, chan_size)
    def _(k):
        to_chan(mixed, place, 6, chan_peer(k))

    place[...] = mixed[...]

    @pl.when(is_owner)
    def _():
        wait_bytes(recv_x.at[pl.ds(0, half)], recv_sems.at[1])
        inputs = spectrum(seq_size, [(1, recv_x.at[late])], lhs, twiddle, middle, first)
        product[...] += multiply(inputs, taps_spectrum[...])
        inverse(
            seq_size, product[...], 1, mid, twiddle, middle, last, send_y.at[late]
        )

        @pl.loop(0, half)
        def _(k):
            p = half + lax.rem(d + k, half)
            to_seq(send_y.at[p], recv_y.at[d], 1, 5, p)

    own_columns.wait()
    rest = pl.ds(0, (chan_size - 1) * chans)
    wait_bytes(columns.at[rest, :], recv_sems.at[4])
    wait_bytes(gathered.at[:, rest], recv_sems.at[6])
    out_ref[...] = dot(gathered[...], columns[...]).astype(out_ref.dtype)

    @pl.when(is_owner)
    def _():
        wait_bytes(send_x.at[pl.ds(0, owners - 1)], send_sems.at[0])
        wait_bytes(send_y.at[pl.ds(0, seq_size - 1)], send_sems.at[1])
        wait_bytes(all_params.at[others], send_sems.at[2])
        wait_bytes(send_taps.at[others], send_sems.at[3])

    @pl.when(jnp.logical_not(is_owner))
    def _():
        wait_bytes(send_x, send_sems.at[0])

    wait_bytes(columns.at[rest, :], send_sems.at[4])
    wait_bytes(gathered.at[:, rest], send_sems.at[6])


def shards(
    mixer_input,
    gate_branch,
    skip_gain,
    decay_rate,
    first_weight,
    first_bias,
    second_weight,
    second_bias,
    last_weight,
    output_weight,
):
    block, chans = mixer_input.shape
    seq_size = lax.axis_size("seq")
    chan_size = lax.axis_size("chan")
    emb, order = first_weight.shape
    feats = output_weight.shape[1] // chan_size
    owners = seq_size // 4
    per = chans // owners
    share = seq_size // chan_size
    length = block * seq_size
    held = [
        mixer_input,
        gate_branch,
        skip_gain.reshape(1, chans),
        decay_rate.reshape(1, chans),
        first_weight,
        first_bias.reshape(1, order),
        second_weight,
        second_bias.reshape(1, order),
        last_weight,
        *[jnp.asarray(table) for table in transform_tables(seq_size, block)],
    ]
    return pl.pallas_call(
        functools.partial(
            mixer_kernel, seq_size, chan_size, owners, band_frequencies(length, emb), len(held)
        ),
        out_shape=jax.ShapeDtypeStruct((block, feats), BF16),
        in_specs=[pl.BlockSpec(memory_space=pltpu.HBM)] * (len(held) + 1),
        out_specs=pl.BlockSpec(memory_space=pltpu.VMEM),
        scratch_shapes=[
            *[pltpu.VMEM(value.shape, value.dtype) for value in held],
            pltpu.VMEM((-(-(emb + 1) // 8) * 8, order), F32),
            pltpu.VMEM((order + 8, order), F32),
            pltpu.VMEM((order + 8, share * block), F32),
            pltpu.VMEM((order, share * block), F32),
            pltpu.VMEM((block, chans), F32),
            pltpu.VMEM((owners, per, block), F32),
            pltpu.VMEM((chan_size, per, block), F32),
            pltpu.VMEM((chan_size, share, per, block), F32),
            pltpu.VMEM((seq_size, per, block), F32),
            pltpu.VMEM((owners, per, block), F32),
            pltpu.VMEM((seq_size, per, block), F32),
            pltpu.VMEM((per * seq_size, 2 * block), F32),
            pltpu.VMEM((per * seq_size, 2 * block), F32),
            pltpu.VMEM((per * seq_size, 2 * block), F32),
            pltpu.VMEM((2 * seq_size, per * block), F32),
            pltpu.VMEM((seq_size, per, block), F32),
            pltpu.VMEM((owners, per, block), F32),
            pltpu.VMEM((block, chans), BF16),
            pltpu.VMEM((block, chan_size * chans), BF16),
            pltpu.VMEM((chan_size * chans, feats), BF16),
            pltpu.SemaphoreType.DMA((7,)),
            pltpu.SemaphoreType.DMA((7,)),
            pltpu.SemaphoreType.DMA((len(held) + 1,)),
        ],
        compiler_params=pltpu.CompilerParams(
            collective_id=0, has_side_effects=True, vmem_limit_bytes=62 << 20
        ),
    )(*held, output_weight)


def solution(mesh):
    in_specs = (
        P("seq", "chan"),
        P("seq", "chan"),
        P("chan"),
        P("chan"),
        P(),
        P(),
        P(),
        P(),
        P(None, "chan"),
        P("chan", None),
    )
    out_specs = P("seq", "chan")
    return jax.shard_map(shards, mesh=mesh, in_specs=in_specs, out_specs=out_specs, check_vma=False)
```

```python
import functools
import math

import jax
import jax.numpy as jnp
import ml_dtypes
import numpy as np
from jax import lax
from jax.experimental import pallas as pl
from jax.experimental.pallas import tpu as pltpu
from jax.sharding import PartitionSpec as P

HIGHEST = lax.Precision.HIGHEST
F32 = jnp.float32
BF16 = jnp.bfloat16
MESH = pl.DeviceIdType.MESH


def band_frequencies(length, emb_width):
    band_count = (emb_width - 1) // 2
    return [
        min(length // 2, max(b, int((length / 2) ** ((b - 1) / (band_count - 1)))))
        for b in range(1, band_count + 1)
    ]


def two_terms(table):
    high = table.astype(np.float32).astype(ml_dtypes.bfloat16)
    low = (table - high.astype(np.float64)).astype(np.float32).astype(ml_dtypes.bfloat16)
    return high, low


def transform_tables(blocks, width):
    length = blocks * width
    k1 = np.arange(blocks)[:, None]
    b = np.arange(blocks)[None, :]
    across = 2.0 * math.pi * (k1 + 0.25) * b / blocks
    first = np.concatenate([np.cos(across), -np.sin(across)], axis=0)
    last = np.concatenate([np.cos(across).T, -np.sin(across).T], axis=1) / length
    j = np.arange(width)
    turn = 2.0 * math.pi * (k1 + 0.25) * j[None, :] / length
    twiddle = np.concatenate([np.cos(turn), np.sin(turn)]).astype(np.float32)
    within = 2.0 * math.pi * ((j[:, None] * j[None, :]) % width) / width
    cos, sin = np.cos(within), np.sin(within)
    middle = np.concatenate(two_terms(np.block([[cos, -sin], [sin, cos]])), axis=0)
    first = np.stack(
        [np.concatenate(two_terms(half) * 2, axis=1) for half in np.split(first, 2, axis=1)]
    )
    last = np.concatenate(two_terms(last), axis=1)
    return twiddle, middle, first, last


def split(value):
    high = value.astype(BF16)
    return high, (value - high.astype(F32)).astype(BF16)


def dot(left, right):
    return jnp.dot(left, right, preferred_element_type=F32)


def dot_nt(left, right):
    return lax.dot_general(left, right, (((1,), (1,)), ((), ())), preferred_element_type=F32)


def contract_first(left, right):
    return lax.dot_general(
        left, right, (((0,), (0,)), ((), ())), precision=HIGHEST, preferred_element_type=F32
    )


def hidden_block(start, length, freqs, width, w1_ref, b1_ref, w2_ref, b2_ref, pad1, pad2, hid, out):
    emb, order = w1_ref.shape
    rows = pad1.shape[0]
    row = lax.broadcasted_iota(jnp.int32, (rows, width), 0)
    time = start + lax.broadcasted_iota(jnp.int32, (rows, width), 1)
    freq = jnp.zeros((rows, width), jnp.int32)
    for band, f in enumerate(freqs):
        freq = jnp.where((row == 2 * band + 1) | (row == 2 * band + 2), f, freq)
    shift = jnp.where(lax.rem(row, 2) == 1, length // 4, 0)
    phase = lax.rem(time * freq + shift, length).astype(F32) * (2.0 * math.pi / length)
    features = jnp.where(row == 0, time.astype(F32) / length, jnp.sin(phase))
    features = jnp.where(row == emb, 1.0, jnp.where(row > emb, 0.0, features))
    pad1[...] = jnp.zeros_like(pad1)
    pad1[0:emb, :] = w1_ref[...]
    pad1[emb : emb + 1, :] = b1_ref[...]
    hid[0:order, :] = jnp.sin(contract_first(pad1[...], features))
    extra = lax.broadcasted_iota(jnp.int32, (hid.shape[0] - order, width), 0)
    hid[order:, :] = jnp.where(extra == 0, 1.0, 0.0)
    pad2[...] = jnp.zeros_like(pad2)
    pad2[0:order, :] = w2_ref[...]
    pad2[order : order + 1, :] = b2_ref[...]
    out[...] = jnp.sin(contract_first(pad2[...], hid[...]))


def filter_taps(start, length, order, params, hidden):
    rate = params[:, order : order + 1]
    shaped = jnp.dot(params[:, :order], hidden, precision=HIGHEST, preferred_element_type=F32)
    small = rate * (-2.0 / length)
    series = jnp.ones_like(small)
    for term in range(8, 1, -1):
        series = 1.0 + series * small * (1.0 / term)
    scale = lax.rsqrt((jnp.exp(-2.0 * rate) - 1.0) / (small * series))
    fraction = (start + lax.broadcasted_iota(jnp.int32, shaped.shape, 1)).astype(F32) / length
    skip = params[:, order + 1 : order + 2]
    return shaped * jnp.exp(-rate * fraction) * scale + jnp.where(fraction == 0.0, skip, 0.0)


def flat(ref):
    return jnp.concatenate([ref[:, i, :] for i in range(ref.shape[1])], axis=1)


def spectrum(blocks, stage, lhs, twiddle, middle):
    width = twiddle.shape[1]
    cos, sin = twiddle[:blocks, :], twiddle[blocks:, :]
    for i in range(stage.shape[1] // width):
        re = stage[:blocks, i * width : (i + 1) * width]
        im = stage[blocks:, i * width : (i + 1) * width]
        lhs[i * blocks : (i + 1) * blocks, :width] = re * cos + im * sin
        lhs[i * blocks : (i + 1) * blocks, width:] = im * cos - re * sin
    table_high, table_low = middle[: 2 * width, :], middle[2 * width :, :]
    high, low = split(lhs[...])
    return dot(high, table_high) + (dot(low, table_high) + dot(high, table_low))


def taps_stage(first, which, ref):
    high, low = split(flat(ref))
    return dot(first[which], jnp.concatenate([high, high, low, low], axis=0))


def input_stage(first, which, ref, wide):
    wide[...] = ref[...].astype(F32)
    value = flat(wide).astype(BF16)
    return dot(first[which, :, : 2 * value.shape[0]], jnp.concatenate([value, value], axis=0))


def multiply(left, right):
    width = left.shape[1] // 2
    left_re, left_im, right_re, right_im = left[:, :width], left[:, width:], right[:, :width], right[:, width:]
    return jnp.concatenate(
        [left_re * right_re - left_im * right_im, left_re * right_im + left_im * right_re], axis=1
    )


def inverse(blocks, product, which, mid, twiddle, middle, last, wide, out):
    width = twiddle.shape[1]
    table_high, table_low = middle[: 2 * width, :], middle[2 * width :, :]
    high, low = split(product)
    stage = dot_nt(high, table_high) + (dot_nt(low, table_high) + dot_nt(high, table_low))
    cos, sin = twiddle[:blocks, :], twiddle[blocks:, :]
    per = out.shape[1]
    for i in range(per):
        re = stage[i * blocks : (i + 1) * blocks, :width]
        im = stage[i * blocks : (i + 1) * blocks, width:]
        mid[:blocks, i * width : (i + 1) * width] = re * cos - im * sin
        mid[blocks:, i * width : (i + 1) * width] = re * sin + im * cos
    high, low = split(mid[...])
    table = last[which * (blocks // 2) : (which + 1) * (blocks // 2), :]
    result = dot(table, jnp.concatenate([high, high], axis=0))
    result += dot(table, jnp.concatenate([low, low], axis=0))
    for i in range(per):
        wide[:, i, :] = result[:, i * width : (i + 1) * width]
    out[...] = wide[...].astype(out.dtype)


def mixer_kernel(seq_size, chan_size, owners, freqs, arrays, *refs):
    sources, weight_hbm, out_ref = refs[:arrays], refs[arrays], refs[arrays + 1]
    held = refs[arrays + 2 : 2 * arrays + 2]
    x_ref, gate_ref, skip_ref, decay_ref, w1_ref, b1_ref, w2_ref, b2_ref, wl_ref = held[:9]
    twiddle, middle, first, last = held[9:]
    (
        pad1,
        pad2,
        hid,
        hidden,
        rows,
        params,
        all_params,
        send_taps,
        recv_taps,
        send_x,
        recv_x,
        lhs,
        taps_spectrum,
        product,
        mid,
        wide,
        send_y,
        recv_y,
        mixed,
        gathered,
        columns,
        send_sems,
        recv_sems,
        local_sems,
    ) = refs[2 * arrays + 2 :]
    block, chans = x_ref.shape
    order = w1_ref.shape[1]
    length = seq_size * block
    half = seq_size // 2
    per = chans // owners
    share = seq_size // chan_size
    feats = out_ref.shape[1]
    d = lax.axis_index("seq")
    c = lax.axis_index("chan")
    base = (half - owners) // 2
    rank = d - base
    is_owner = (rank >= 0) & (rank < owners)

    def chan_peer(k):
        return lax.rem(c + k, chan_size)

    def wait_bytes(ref, sem):
        pltpu.make_async_copy(ref, ref, sem).wait()

    def to_seq(source, target, lane, landing, p):
        pltpu.make_async_remote_copy(
            src_ref=source,
            dst_ref=target,
            send_sem=send_sems.at[lane],
            recv_sem=recv_sems.at[landing],
            device_id={"seq": p},
            device_id_type=MESH,
        ).start()

    def to_chan(source, target, lane, p):
        pltpu.make_async_remote_copy(
            src_ref=source,
            dst_ref=target,
            send_sem=send_sems.at[lane],
            recv_sem=recv_sems.at[lane],
            device_id={"chan": p},
            device_id_type=MESH,
        ).start()

    loads = [
        pltpu.make_async_copy(source, target, local_sems.at[i])
        for i, (source, target) in enumerate(zip(sources, held))
    ]
    for load in loads:
        load.start()
    barrier = pltpu.get_barrier_semaphore()

    @pl.when(is_owner)
    def _():
        @pl.loop(1, seq_size)
        def _(k):
            p = lax.rem(d + k, seq_size)
            pl.semaphore_signal(barrier, inc=1, device_id={"seq": p}, device_id_type=MESH)

    @pl.loop(1, chan_size)
    def _(k):
        pl.semaphore_signal(
            barrier, inc=1, device_id={"chan": chan_peer(k)}, device_id_type=MESH
        )

    own_columns = pltpu.make_async_copy(
        weight_hbm.at[:, pl.ds(pl.multiple_of(c * feats, feats), feats)],
        columns.at[pl.ds(pl.multiple_of(c * chans, chans), chans), :],
        local_sems.at[arrays],
    )
    own_columns.start()
    for load in loads:
        load.wait()

    send_x[...] = x_ref[...].astype(F32).T.reshape(owners, per, block).astype(BF16)

    @pl.when(is_owner)
    def _():
        rows[...] = jnp.zeros_like(rows)
        rows[:order, :] = wl_ref[...]
        rows[order : order + 1, :] = decay_ref[...]
        rows[order + 1 : order + 2, :] = skip_ref[...]
        params[...] = rows[...].T.reshape(owners, per, block)
        pl.semaphore_wait(barrier, owners - 1 + chan_size - 1)

    @pl.when(jnp.logical_not(is_owner))
    def _():
        pl.semaphore_wait(barrier, owners + chan_size - 1)

    @pl.loop(0, owners)
    def _(o):
        @pl.when(o != rank)
        def _():
            to_seq(send_x.at[o], recv_x.at[d], 0, jnp.where(d < half, 0, 1), base + o)

    others = pl.ds(0, (chan_size - 1))

    @pl.when(is_owner)
    def _():
        @pl.loop(1, chan_size)
        def _(k):
            to_chan(params.at[rank], all_params.at[c], 2, chan_peer(k))

        all_params[c] = params[rank]
        recv_x[d] = send_x[rank]
        start = c * (share * block)
        hidden_block(
            start,
            length,
            freqs,
            share * block,
            w1_ref,
            b1_ref,
            w2_ref,
            b2_ref,
            pad1,
            pad2,
            hid,
            hidden,
        )
        wait_bytes(all_params.at[others], recv_sems.at[2])
        taps = filter_taps(
            start, length, order, all_params[...].reshape(chan_size * per, block), hidden[...]
        )
        for q in range(share):
            send_taps[:, q] = taps[:, q * block : (q + 1) * block].reshape(chan_size, per, block)
        here = pl.ds(c * share, share)

        @pl.loop(1, chan_size)
        def _(k):
            p = chan_peer(k)
            to_chan(send_taps.at[p], recv_taps.at[here], 3, p)

        recv_taps[here] = send_taps[c]

    @pl.loop(1, chan_size)
    def _(k):
        p = chan_peer(k)
        to_chan(
            weight_hbm.at[:, pl.ds(pl.multiple_of(p * feats, feats), feats)],
            columns.at[pl.ds(pl.multiple_of(c * chans, chans), chans), :],
            4,
            p,
        )

    early, late = pl.ds(0, half), pl.ds(half, half)

    @pl.when(is_owner)
    def _():
        wait_bytes(recv_taps.at[pl.ds(0, (chan_size - 1) * share)], recv_sems.at[3])
        stage = taps_stage(first, 0, recv_taps.at[early]) + taps_stage(first, 1, recv_taps.at[late])
        taps_spectrum[...] = spectrum(seq_size, stage, lhs, twiddle, middle)
        wait_bytes(recv_x.at[pl.ds(0, half - 1)], recv_sems.at[0])
        stage = input_stage(first, 0, recv_x.at[early], wide)
        inputs = spectrum(seq_size, stage, lhs, twiddle, middle)
        product[...] = multiply(inputs, taps_spectrum[...])
        inverse(
            seq_size, product[...], 0, mid, twiddle, middle, last, wide, send_y.at[early]
        )

        @pl.loop(1, half)
        def _(k):
            p = lax.rem(d + k, half)
            to_seq(send_y.at[p], recv_y.at[rank], 1, 5, p)

        recv_y[rank] = send_y[d]
        wait_bytes(recv_y.at[pl.ds(0, owners - 1)], recv_sems.at[5])

    @pl.when(jnp.logical_not(is_owner))
    def _():
        wait_bytes(recv_y, recv_sems.at[5])

    convolved = recv_y[...].astype(F32).reshape(chans, block).T
    mixed[...] = (gate_ref[...].astype(F32) * convolved).astype(BF16)
    place = gathered.at[:, pl.ds(pl.multiple_of(c * chans, chans), chans)]

    @pl.loop(1, chan_size)
    def _(k):
        to_chan(mixed, place, 6, chan_peer(k))

    place[...] = mixed[...]

    @pl.when(is_owner)
    def _():
        wait_bytes(recv_x.at[pl.ds(0, half)], recv_sems.at[1])
        stage = input_stage(first, 1, recv_x.at[late], wide)
        inputs = spectrum(seq_size, stage, lhs, twiddle, middle)
        product[...] += multiply(inputs, taps_spectrum[...])
        inverse(
            seq_size, product[...], 1, mid, twiddle, middle, last, wide, send_y.at[late]
        )

        @pl.loop(0, half)
        def _(k):
            p = half + lax.rem(d + k, half)
            to_seq(send_y.at[p], recv_y.at[rank], 1, 5, p)

    own_columns.wait()
    rest = pl.ds(0, (chan_size - 1) * chans)
    wait_bytes(columns.at[rest, :], recv_sems.at[4])
    wait_bytes(gathered.at[:, rest], recv_sems.at[6])
    out_ref[...] = dot(gathered[...], columns[...]).astype(out_ref.dtype)

    @pl.when(is_owner)
    def _():
        wait_bytes(send_x.at[pl.ds(0, owners - 1)], send_sems.at[0])
        wait_bytes(send_y.at[pl.ds(0, seq_size - 1)], send_sems.at[1])
        wait_bytes(all_params.at[others], send_sems.at[2])
        wait_bytes(send_taps.at[others], send_sems.at[3])

    @pl.when(jnp.logical_not(is_owner))
    def _():
        wait_bytes(send_x, send_sems.at[0])

    wait_bytes(columns.at[rest, :], send_sems.at[4])
    wait_bytes(gathered.at[:, rest], send_sems.at[6])


def shards(
    mixer_input,
    gate_branch,
    skip_gain,
    decay_rate,
    first_weight,
    first_bias,
    second_weight,
    second_bias,
    last_weight,
    output_weight,
):
    block, chans = mixer_input.shape
    seq_size = lax.axis_size("seq")
    chan_size = lax.axis_size("chan")
    emb, order = first_weight.shape
    feats = output_weight.shape[1] // chan_size
    owners = seq_size // 4
    per = chans // owners
    share = seq_size // chan_size
    length = block * seq_size
    held = [
        mixer_input,
        gate_branch,
        skip_gain.reshape(1, chans),
        decay_rate.reshape(1, chans),
        first_weight,
        first_bias.reshape(1, order),
        second_weight,
        second_bias.reshape(1, order),
        last_weight,
        *[jnp.asarray(table) for table in transform_tables(seq_size, block)],
    ]
    return pl.pallas_call(
        functools.partial(
            mixer_kernel, seq_size, chan_size, owners, band_frequencies(length, emb), len(held)
        ),
        out_shape=jax.ShapeDtypeStruct((block, feats), BF16),
        in_specs=[pl.BlockSpec(memory_space=pltpu.HBM)] * (len(held) + 1),
        out_specs=pl.BlockSpec(memory_space=pltpu.VMEM),
        scratch_shapes=[
            *[pltpu.VMEM(value.shape, value.dtype) for value in held],
            pltpu.VMEM((-(-(emb + 1) // 8) * 8, order), F32),
            pltpu.VMEM((order + 8, order), F32),
            pltpu.VMEM((order + 8, share * block), F32),
            pltpu.VMEM((order, share * block), F32),
            pltpu.VMEM((block, chans), F32),
            pltpu.VMEM((owners, per, block), F32),
            pltpu.VMEM((chan_size, per, block), F32),
            pltpu.VMEM((chan_size, share, per, block), F32),
            pltpu.VMEM((seq_size, per, block), F32),
            pltpu.VMEM((owners, per, block), BF16),
            pltpu.VMEM((seq_size, per, block), BF16),
            pltpu.VMEM((per * seq_size, 2 * block), F32),
            pltpu.VMEM((per * seq_size, 2 * block), F32),
            pltpu.VMEM((per * seq_size, 2 * block), F32),
            pltpu.VMEM((2 * seq_size, per * block), F32),
            pltpu.VMEM((seq_size // 2, per, block), F32),
            pltpu.VMEM((seq_size, per, block), BF16),
            pltpu.VMEM((owners, per, block), BF16),
            pltpu.VMEM((block, chans), BF16),
            pltpu.VMEM((block, chan_size * chans), BF16),
            pltpu.VMEM((chan_size * chans, feats), BF16),
            pltpu.SemaphoreType.DMA((7,)),
            pltpu.SemaphoreType.DMA((7,)),
            pltpu.SemaphoreType.DMA((len(held) + 1,)),
        ],
        compiler_params=pltpu.CompilerParams(
            collective_id=0, has_side_effects=True, vmem_limit_bytes=62 << 20
        ),
    )(*held, output_weight)


def solution(mesh):
    in_specs = (
        P("seq", "chan"),
        P("seq", "chan"),
        P("chan"),
        P("chan"),
        P(),
        P(),
        P(),
        P(),
        P(None, "chan"),
        P("chan", None),
    )
    out_specs = P("seq", "chan")
    return jax.shard_map(shards, mesh=mesh, in_specs=in_specs, out_specs=out_specs, check_vma=False)
```

```python
import functools
import math

import jax
import jax.numpy as jnp
import ml_dtypes
import numpy as np
from jax import lax
from jax.experimental import pallas as pl
from jax.experimental.pallas import tpu as pltpu
from jax.sharding import PartitionSpec as P

HIGHEST = lax.Precision.HIGHEST
F32 = jnp.float32
BF16 = jnp.bfloat16
MESH = pl.DeviceIdType.MESH


def band_frequencies(length, emb_width):
    band_count = (emb_width - 1) // 2
    return [
        min(length // 2, max(b, int((length / 2) ** ((b - 1) / (band_count - 1)))))
        for b in range(1, band_count + 1)
    ]


def two_terms(table):
    high = table.astype(np.float32).astype(ml_dtypes.bfloat16)
    low = (table - high.astype(np.float64)).astype(np.float32).astype(ml_dtypes.bfloat16)
    return high, low


def transform_tables(blocks, width):
    length = blocks * width
    k1 = np.arange(blocks)[:, None]
    b = np.arange(blocks)[None, :]
    across = 2.0 * math.pi * (k1 + 0.25) * b / blocks
    first = np.concatenate([np.cos(across), -np.sin(across)], axis=0)
    last = np.concatenate([np.cos(across).T, -np.sin(across).T], axis=1) / length
    j = np.arange(width)
    turn = 2.0 * math.pi * (k1 + 0.25) * j[None, :] / length
    twiddle = np.concatenate([np.cos(turn), np.sin(turn)]).astype(np.float32)
    within = 2.0 * math.pi * ((j[:, None] * j[None, :]) % width) / width
    cos, sin = np.cos(within), np.sin(within)
    middle = np.concatenate(two_terms(np.block([[cos, -sin], [sin, cos]])), axis=0)
    first = np.stack(
        [np.concatenate(two_terms(half) * 2, axis=1) for half in np.split(first, 2, axis=1)]
    )
    last = np.concatenate(two_terms(last), axis=1)
    return twiddle, middle, first, last


def split(value):
    high = value.astype(BF16)
    return high, (value - high.astype(F32)).astype(BF16)


def dot(left, right):
    return jnp.dot(left, right, preferred_element_type=F32)


def dot_nt(left, right):
    return lax.dot_general(left, right, (((1,), (1,)), ((), ())), preferred_element_type=F32)


def contract_first(left, right):
    return lax.dot_general(
        left, right, (((0,), (0,)), ((), ())), precision=HIGHEST, preferred_element_type=F32
    )


def hidden_block(start, length, freqs, width, w1_ref, b1_ref, w2_ref, b2_ref, pad1, pad2, hid, out):
    emb, order = w1_ref.shape
    rows = pad1.shape[0]
    row = lax.broadcasted_iota(jnp.int32, (rows, width), 0)
    time = start + lax.broadcasted_iota(jnp.int32, (rows, width), 1)
    freq = jnp.zeros((rows, width), jnp.int32)
    for band, f in enumerate(freqs):
        freq = jnp.where((row == 2 * band + 1) | (row == 2 * band + 2), f, freq)
    shift = jnp.where(lax.rem(row, 2) == 1, length // 4, 0)
    phase = lax.rem(time * freq + shift, length).astype(F32) * (2.0 * math.pi / length)
    features = jnp.where(row == 0, time.astype(F32) / length, jnp.sin(phase))
    features = jnp.where(row == emb, 1.0, jnp.where(row > emb, 0.0, features))
    pad1[...] = jnp.zeros_like(pad1)
    pad1[0:emb, :] = w1_ref[...]
    pad1[emb : emb + 1, :] = b1_ref[...]
    hid[0:order, :] = jnp.sin(contract_first(pad1[...], features))
    extra = lax.broadcasted_iota(jnp.int32, (hid.shape[0] - order, width), 0)
    hid[order:, :] = jnp.where(extra == 0, 1.0, 0.0)
    pad2[...] = jnp.zeros_like(pad2)
    pad2[0:order, :] = w2_ref[...]
    pad2[order : order + 1, :] = b2_ref[...]
    out[...] = jnp.sin(contract_first(pad2[...], hid[...]))


def filter_taps(start, length, order, params, hidden):
    rate = params[:, order : order + 1]
    shaped = jnp.dot(params[:, :order], hidden, precision=HIGHEST, preferred_element_type=F32)
    small = rate * (-2.0 / length)
    series = jnp.ones_like(small)
    for term in range(8, 1, -1):
        series = 1.0 + series * small * (1.0 / term)
    scale = lax.rsqrt((jnp.exp(-2.0 * rate) - 1.0) / (small * series))
    fraction = (start + lax.broadcasted_iota(jnp.int32, shaped.shape, 1)).astype(F32) / length
    skip = params[:, order + 1 : order + 2]
    return shaped * jnp.exp(-rate * fraction) * scale + jnp.where(fraction == 0.0, skip, 0.0)


def flat(ref):
    return jnp.concatenate([ref[:, i, :] for i in range(ref.shape[1])], axis=1)


def spectrum(blocks, stage, lhs, twiddle, middle):
    width = twiddle.shape[1]
    cos, sin = twiddle[:blocks, :], twiddle[blocks:, :]
    for i in range(stage.shape[1] // width):
        re = stage[:blocks, i * width : (i + 1) * width]
        im = stage[blocks:, i * width : (i + 1) * width]
        lhs[i * blocks : (i + 1) * blocks, :width] = re * cos + im * sin
        lhs[i * blocks : (i + 1) * blocks, width:] = im * cos - re * sin
    table_high, table_low = middle[: 2 * width, :], middle[2 * width :, :]
    high, low = split(lhs[...])
    return dot(high, table_high) + (dot(low, table_high) + dot(high, table_low))


def taps_stage(first, which, ref):
    high, low = split(flat(ref))
    return dot(first[which], jnp.concatenate([high, high, low, low], axis=0))


def input_stage(first, which, ref, wide):
    wide[...] = ref[...].astype(F32)
    value = flat(wide).astype(BF16)
    return dot(first[which, :, : 2 * value.shape[0]], jnp.concatenate([value, value], axis=0))


def multiply(left, right):
    width = left.shape[1] // 2
    left_re, left_im, right_re, right_im = left[:, :width], left[:, width:], right[:, :width], right[:, width:]
    return jnp.concatenate(
        [left_re * right_re - left_im * right_im, left_re * right_im + left_im * right_re], axis=1
    )


def inverse(blocks, product, which, mid, twiddle, middle, last, wide, out):
    width = twiddle.shape[1]
    table_high, table_low = middle[: 2 * width, :], middle[2 * width :, :]
    high, low = split(product)
    stage = dot_nt(high, table_high) + (dot_nt(low, table_high) + dot_nt(high, table_low))
    cos, sin = twiddle[:blocks, :], twiddle[blocks:, :]
    per = out.shape[1]
    for i in range(per):
        re = stage[i * blocks : (i + 1) * blocks, :width]
        im = stage[i * blocks : (i + 1) * blocks, width:]
        mid[:blocks, i * width : (i + 1) * width] = re * cos - im * sin
        mid[blocks:, i * width : (i + 1) * width] = re * sin + im * cos
    high, low = split(mid[...])
    table = last[which * (blocks // 2) : (which + 1) * (blocks // 2), :]
    result = dot(table, jnp.concatenate([high, high], axis=0))
    result += dot(table, jnp.concatenate([low, low], axis=0))
    for i in range(per):
        wide[:, i, :] = result[:, i * width : (i + 1) * width]
    out[...] = wide[...].astype(out.dtype)


def mixer_kernel(seq_size, chan_size, owners, freqs, arrays, *refs):
    sources, weight_hbm, out_ref = refs[:arrays], refs[arrays], refs[arrays + 1]
    held = refs[arrays + 2 : 2 * arrays + 2]
    x_ref, gate_ref, skip_ref, decay_ref, w1_ref, b1_ref, w2_ref, b2_ref, wl_ref = held[:9]
    twiddle, middle, first, last = held[9:]
    (
        pad1,
        pad2,
        hid,
        hidden,
        rows,
        params,
        all_params,
        send_taps,
        recv_taps,
        send_x,
        recv_x,
        lhs,
        taps_spectrum,
        product,
        mid,
        wide,
        send_y,
        recv_y,
        mixed,
        gathered,
        columns,
        send_sems,
        recv_sems,
        local_sems,
    ) = refs[2 * arrays + 2 :]
    block, chans = x_ref.shape
    order = w1_ref.shape[1]
    length = seq_size * block
    half = seq_size // 2
    per = chans // owners
    share = seq_size // chan_size
    feats = out_ref.shape[1]
    d = lax.axis_index("seq")
    c = lax.axis_index("chan")
    base = (half - owners) // 2
    rank = d - base
    is_owner = (rank >= 0) & (rank < owners)
    core = lax.rem(d, 2)
    sibling = d + 1 - 2 * core
    part = chans // 2

    def chan_peer(k):
        return lax.rem(c + k, chan_size)

    def wait_bytes(ref, sem):
        pltpu.make_async_copy(ref, ref, sem).wait()

    def to_seq(source, target, lane, landing, p):
        pltpu.make_async_remote_copy(
            src_ref=source,
            dst_ref=target,
            send_sem=send_sems.at[lane],
            recv_sem=recv_sems.at[landing],
            device_id={"seq": p},
            device_id_type=MESH,
        ).start()

    def to_chan(source, target, lane, p):
        pltpu.make_async_remote_copy(
            src_ref=source,
            dst_ref=target,
            send_sem=send_sems.at[lane],
            recv_sem=recv_sems.at[lane],
            device_id={"chan": p},
            device_id_type=MESH,
        ).start()

    loads = [
        pltpu.make_async_copy(source, target, local_sems.at[i])
        for i, (source, target) in enumerate(zip(sources, held))
    ]
    for load in loads:
        load.start()
    barrier = pltpu.get_barrier_semaphore()

    @pl.when(is_owner)
    def _():
        @pl.loop(1, seq_size)
        def _(k):
            p = lax.rem(d + k, seq_size)
            pl.semaphore_signal(barrier, inc=1, device_id={"seq": p}, device_id_type=MESH)

    @pl.when(jnp.logical_not(is_owner))
    def _():
        pl.semaphore_signal(barrier, inc=1, device_id={"seq": sibling}, device_id_type=MESH)

    @pl.loop(1, chan_size)
    def _(k):
        pl.semaphore_signal(
            barrier, inc=1, device_id={"chan": chan_peer(k)}, device_id_type=MESH
        )

    def weight_part(p):
        return weight_hbm.at[
            pl.ds(pl.multiple_of(core * part, part), part),
            pl.ds(pl.multiple_of(p * feats, feats), feats),
        ]

    own_columns = pltpu.make_async_copy(
        weight_part(c),
        columns.at[c, core],
        local_sems.at[arrays],
    )
    own_columns.start()
    for load in loads:
        load.wait()

    send_x[...] = x_ref[...].astype(F32).T.reshape(owners, per, block).astype(BF16)

    @pl.when(is_owner)
    def _():
        rows[...] = jnp.zeros_like(rows)
        rows[:order, :] = wl_ref[...]
        rows[order : order + 1, :] = decay_ref[...]
        rows[order + 1 : order + 2, :] = skip_ref[...]
        params[...] = rows[...].T.reshape(owners, per, block)
        pl.semaphore_wait(barrier, owners - 1 + chan_size - 1)

    @pl.when(jnp.logical_not(is_owner))
    def _():
        pl.semaphore_wait(barrier, owners + 1 + chan_size - 1)

    @pl.loop(0, owners)
    def _(o):
        @pl.when(o != rank)
        def _():
            to_seq(send_x.at[o], recv_x.at[d], 0, jnp.where(d < half, 0, 1), base + o)

    others = pl.ds(0, (chan_size - 1))

    @pl.when(is_owner)
    def _():
        @pl.loop(1, chan_size)
        def _(k):
            to_chan(params.at[rank], all_params.at[c], 2, chan_peer(k))

        all_params[c] = params[rank]
        recv_x[d] = send_x[rank]
        start = c * (share * block)
        hidden_block(
            start,
            length,
            freqs,
            share * block,
            w1_ref,
            b1_ref,
            w2_ref,
            b2_ref,
            pad1,
            pad2,
            hid,
            hidden,
        )
        wait_bytes(all_params.at[others], recv_sems.at[2])
        taps = filter_taps(
            start, length, order, all_params[...].reshape(chan_size * per, block), hidden[...]
        )
        for q in range(share):
            send_taps[:, q] = taps[:, q * block : (q + 1) * block].reshape(chan_size, per, block)
        here = pl.ds(c * share, share)

        @pl.loop(1, chan_size)
        def _(k):
            p = chan_peer(k)
            to_chan(send_taps.at[p], recv_taps.at[here], 3, p)

        recv_taps[here] = send_taps[c]

    @pl.loop(1, chan_size)
    def _(k):
        p = chan_peer(k)
        to_chan(weight_part(p), columns.at[c, core], 4, p)

    def share_weights():
        own_columns.wait()
        wait_bytes(columns.at[others, 0], recv_sems.at[4])
        to_seq(columns.at[:, core], columns.at[:, core], 5, 7, sibling)

    early, late = pl.ds(0, half), pl.ds(half, half)

    @pl.when(is_owner)
    def _():
        wait_bytes(recv_taps.at[pl.ds(0, (chan_size - 1) * share)], recv_sems.at[3])
        stage = taps_stage(first, 0, recv_taps.at[early]) + taps_stage(first, 1, recv_taps.at[late])
        taps_spectrum[...] = spectrum(seq_size, stage, lhs, twiddle, middle)
        wait_bytes(recv_x.at[pl.ds(0, half - 1)], recv_sems.at[0])
        stage = input_stage(first, 0, recv_x.at[early], wide)
        inputs = spectrum(seq_size, stage, lhs, twiddle, middle)
        product[...] = multiply(inputs, taps_spectrum[...])
        inverse(
            seq_size, product[...], 0, mid, twiddle, middle, last, wide, send_y.at[early]
        )

        @pl.loop(1, half)
        def _(k):
            p = lax.rem(d + k, half)
            to_seq(send_y.at[p], recv_y.at[rank], 1, 5, p)

        recv_y[rank] = send_y[d]
        wait_bytes(recv_y.at[pl.ds(0, owners - 1)], recv_sems.at[5])

    @pl.when(jnp.logical_not(is_owner))
    def _():
        share_weights()
        wait_bytes(recv_y, recv_sems.at[5])

    convolved = recv_y[...].astype(F32).reshape(chans, block).T
    mixed[...] = (gate_ref[...].astype(F32) * convolved).astype(BF16)
    place = gathered.at[:, pl.ds(pl.multiple_of(c * chans, chans), chans)]

    @pl.loop(1, chan_size)
    def _(k):
        to_chan(mixed, place, 6, chan_peer(k))

    place[...] = mixed[...]

    @pl.when(is_owner)
    def _():
        share_weights()
        wait_bytes(recv_x.at[pl.ds(0, half)], recv_sems.at[1])
        stage = input_stage(first, 1, recv_x.at[late], wide)
        inputs = spectrum(seq_size, stage, lhs, twiddle, middle)
        product[...] += multiply(inputs, taps_spectrum[...])
        inverse(
            seq_size, product[...], 1, mid, twiddle, middle, last, wide, send_y.at[late]
        )

        @pl.loop(0, half)
        def _(k):
            p = half + lax.rem(d + k, half)
            to_seq(send_y.at[p], recv_y.at[rank], 1, 5, p)

    rest = pl.ds(0, (chan_size - 1) * chans)
    wait_bytes(columns.at[:, 0], recv_sems.at[7])
    wait_bytes(gathered.at[:, rest], recv_sems.at[6])
    weights = columns[...].reshape(chan_size * chans, feats)
    out_ref[...] = dot(gathered[...], weights).astype(out_ref.dtype)

    @pl.when(is_owner)
    def _():
        wait_bytes(send_x.at[pl.ds(0, owners - 1)], send_sems.at[0])
        wait_bytes(send_y.at[pl.ds(0, seq_size - 1)], send_sems.at[1])
        wait_bytes(all_params.at[others], send_sems.at[2])
        wait_bytes(send_taps.at[others], send_sems.at[3])

    @pl.when(jnp.logical_not(is_owner))
    def _():
        wait_bytes(send_x, send_sems.at[0])

    wait_bytes(columns.at[others, 0], send_sems.at[4])
    wait_bytes(columns.at[:, 0], send_sems.at[5])
    wait_bytes(gathered.at[:, rest], send_sems.at[6])


def shards(
    mixer_input,
    gate_branch,
    skip_gain,
    decay_rate,
    first_weight,
    first_bias,
    second_weight,
    second_bias,
    last_weight,
    output_weight,
):
    block, chans = mixer_input.shape
    seq_size = lax.axis_size("seq")
    chan_size = lax.axis_size("chan")
    emb, order = first_weight.shape
    feats = output_weight.shape[1] // chan_size
    owners = seq_size // 4
    per = chans // owners
    share = seq_size // chan_size
    length = block * seq_size
    held = [
        mixer_input,
        gate_branch,
        skip_gain.reshape(1, chans),
        decay_rate.reshape(1, chans),
        first_weight,
        first_bias.reshape(1, order),
        second_weight,
        second_bias.reshape(1, order),
        last_weight,
        *[jnp.asarray(table) for table in transform_tables(seq_size, block)],
    ]
    return pl.pallas_call(
        functools.partial(
            mixer_kernel, seq_size, chan_size, owners, band_frequencies(length, emb), len(held)
        ),
        out_shape=jax.ShapeDtypeStruct((block, feats), BF16),
        in_specs=[pl.BlockSpec(memory_space=pltpu.HBM)] * (len(held) + 1),
        out_specs=pl.BlockSpec(memory_space=pltpu.VMEM),
        scratch_shapes=[
            *[pltpu.VMEM(value.shape, value.dtype) for value in held],
            pltpu.VMEM((-(-(emb + 1) // 8) * 8, order), F32),
            pltpu.VMEM((order + 8, order), F32),
            pltpu.VMEM((order + 8, share * block), F32),
            pltpu.VMEM((order, share * block), F32),
            pltpu.VMEM((block, chans), F32),
            pltpu.VMEM((owners, per, block), F32),
            pltpu.VMEM((chan_size, per, block), F32),
            pltpu.VMEM((chan_size, share, per, block), F32),
            pltpu.VMEM((seq_size, per, block), F32),
            pltpu.VMEM((owners, per, block), BF16),
            pltpu.VMEM((seq_size, per, block), BF16),
            pltpu.VMEM((per * seq_size, 2 * block), F32),
            pltpu.VMEM((per * seq_size, 2 * block), F32),
            pltpu.VMEM((per * seq_size, 2 * block), F32),
            pltpu.VMEM((2 * seq_size, per * block), F32),
            pltpu.VMEM((seq_size // 2, per, block), F32),
            pltpu.VMEM((seq_size, per, block), BF16),
            pltpu.VMEM((owners, per, block), BF16),
            pltpu.VMEM((block, chans), BF16),
            pltpu.VMEM((block, chan_size * chans), BF16),
            pltpu.VMEM((chan_size, 2, chans // 2, feats), BF16),
            pltpu.SemaphoreType.DMA((7,)),
            pltpu.SemaphoreType.DMA((8,)),
            pltpu.SemaphoreType.DMA((len(held) + 1,)),
        ],
        compiler_params=pltpu.CompilerParams(
            collective_id=0, has_side_effects=True, vmem_limit_bytes=62 << 20
        ),
    )(*held, output_weight)


def solution(mesh):
    in_specs = (
        P("seq", "chan"),
        P("seq", "chan"),
        P("chan"),
        P("chan"),
        P(),
        P(),
        P(),
        P(),
        P(None, "chan"),
        P("chan", None),
    )
    out_specs = P("seq", "chan")
    return jax.shard_map(shards, mesh=mesh, in_specs=in_specs, out_specs=out_specs, check_vma=False)
```

```python
import functools
import math

import jax
import jax.numpy as jnp
import ml_dtypes
import numpy as np
from jax import lax
from jax.experimental import pallas as pl
from jax.experimental.pallas import tpu as pltpu
from jax.sharding import PartitionSpec as P

HIGHEST = lax.Precision.HIGHEST
F32 = jnp.float32
BF16 = jnp.bfloat16
MESH = pl.DeviceIdType.MESH


def band_frequencies(length, emb_width):
    band_count = (emb_width - 1) // 2
    return [
        min(length // 2, max(b, int((length / 2) ** ((b - 1) / (band_count - 1)))))
        for b in range(1, band_count + 1)
    ]


def two_terms(table):
    high = table.astype(np.float32).astype(ml_dtypes.bfloat16)
    low = (table - high.astype(np.float64)).astype(np.float32).astype(ml_dtypes.bfloat16)
    return high, low


def transform_tables(blocks, width):
    length = blocks * width
    k1 = np.arange(blocks)[:, None]
    b = np.arange(blocks)[None, :]
    across = 2.0 * math.pi * (k1 + 0.25) * b / blocks
    first = np.concatenate([np.cos(across), -np.sin(across)], axis=0)
    last = np.concatenate([np.cos(across).T, -np.sin(across).T], axis=1) / length
    j = np.arange(width)
    turn = 2.0 * math.pi * (k1 + 0.25) * j[None, :] / length
    twiddle = np.concatenate([np.cos(turn), np.sin(turn)]).astype(np.float32)
    within = 2.0 * math.pi * ((j[:, None] * j[None, :]) % width) / width
    cos, sin = np.cos(within), np.sin(within)
    middle = np.concatenate(two_terms(np.block([[cos, -sin], [sin, cos]])), axis=0)
    first = np.stack(
        [np.concatenate(two_terms(half) * 2, axis=1) for half in np.split(first, 2, axis=1)]
    )
    last = np.concatenate(two_terms(last), axis=1)
    return twiddle, middle, first, last


def split(value):
    high = value.astype(BF16)
    return high, (value - high.astype(F32)).astype(BF16)


def dot(left, right):
    return jnp.dot(left, right, preferred_element_type=F32)


def dot_nt(left, right):
    return lax.dot_general(left, right, (((1,), (1,)), ((), ())), preferred_element_type=F32)


def contract_first(left, right):
    return lax.dot_general(
        left, right, (((0,), (0,)), ((), ())), precision=HIGHEST, preferred_element_type=F32
    )


def hidden_block(start, length, freqs, width, w1_ref, b1_ref, w2_ref, b2_ref, pad1, pad2, hid, out):
    emb, order = w1_ref.shape
    rows = pad1.shape[0]
    row = lax.broadcasted_iota(jnp.int32, (rows, width), 0)
    time = start + lax.broadcasted_iota(jnp.int32, (rows, width), 1)
    freq = jnp.zeros((rows, width), jnp.int32)
    for band, f in enumerate(freqs):
        freq = jnp.where((row == 2 * band + 1) | (row == 2 * band + 2), f, freq)
    shift = jnp.where(lax.rem(row, 2) == 1, length // 4, 0)
    phase = lax.rem(time * freq + shift, length).astype(F32) * (2.0 * math.pi / length)
    features = jnp.where(row == 0, time.astype(F32) / length, jnp.sin(phase))
    features = jnp.where(row == emb, 1.0, jnp.where(row > emb, 0.0, features))
    pad1[...] = jnp.zeros_like(pad1)
    pad1[0:emb, :] = w1_ref[...]
    pad1[emb : emb + 1, :] = b1_ref[...]
    hid[0:order, :] = jnp.sin(contract_first(pad1[...], features))
    extra = lax.broadcasted_iota(jnp.int32, (hid.shape[0] - order, width), 0)
    hid[order:, :] = jnp.where(extra == 0, 1.0, 0.0)
    pad2[...] = jnp.zeros_like(pad2)
    pad2[0:order, :] = w2_ref[...]
    pad2[order : order + 1, :] = b2_ref[...]
    out[...] = jnp.sin(contract_first(pad2[...], hid[...]))


def filter_taps(start, length, order, params, hidden):
    rate = params[:, order : order + 1]
    shaped = jnp.dot(params[:, :order], hidden, precision=HIGHEST, preferred_element_type=F32)
    small = rate * (-2.0 / length)
    series = jnp.ones_like(small)
    for term in range(8, 1, -1):
        series = 1.0 + series * small * (1.0 / term)
    scale = lax.rsqrt((jnp.exp(-2.0 * rate) - 1.0) / (small * series))
    fraction = (start + lax.broadcasted_iota(jnp.int32, shaped.shape, 1)).astype(F32) / length
    skip = params[:, order + 1 : order + 2]
    return shaped * jnp.exp(-rate * fraction) * scale + jnp.where(fraction == 0.0, skip, 0.0)


def flat(ref):
    return jnp.concatenate([ref[:, i, :] for i in range(ref.shape[1])], axis=1)


def spectrum(blocks, stage, lhs, twiddle, middle):
    width = twiddle.shape[1]
    cos, sin = twiddle[:blocks, :], twiddle[blocks:, :]
    for i in range(stage.shape[1] // width):
        re = stage[:blocks, i * width : (i + 1) * width]
        im = stage[blocks:, i * width : (i + 1) * width]
        lhs[i * blocks : (i + 1) * blocks, :width] = re * cos + im * sin
        lhs[i * blocks : (i + 1) * blocks, width:] = im * cos - re * sin
    table_high, table_low = middle[: 2 * width, :], middle[2 * width :, :]
    high, low = split(lhs[...])
    return dot(high, table_high) + (dot(low, table_high) + dot(high, table_low))


def taps_stage(first, which, ref):
    high, low = split(flat(ref))
    return dot(first[which], jnp.concatenate([high, high, low, low], axis=0))


def input_stage(first, which, ref, wide):
    wide[...] = ref[...].astype(F32)
    value = flat(wide).astype(BF16)
    return dot(first[which, :, : 2 * value.shape[0]], jnp.concatenate([value, value], axis=0))


def multiply(left, right):
    width = left.shape[1] // 2
    left_re, left_im, right_re, right_im = left[:, :width], left[:, width:], right[:, :width], right[:, width:]
    return jnp.concatenate(
        [left_re * right_re - left_im * right_im, left_re * right_im + left_im * right_re], axis=1
    )


def inverse(blocks, product, which, mid, twiddle, middle, last, wide, out):
    width = twiddle.shape[1]
    table_high, table_low = middle[: 2 * width, :], middle[2 * width :, :]
    high, low = split(product)
    stage = dot_nt(high, table_high) + (dot_nt(low, table_high) + dot_nt(high, table_low))
    cos, sin = twiddle[:blocks, :], twiddle[blocks:, :]
    per = out.shape[1]
    for i in range(per):
        re = stage[i * blocks : (i + 1) * blocks, :width]
        im = stage[i * blocks : (i + 1) * blocks, width:]
        mid[:blocks, i * width : (i + 1) * width] = re * cos - im * sin
        mid[blocks:, i * width : (i + 1) * width] = re * sin + im * cos
    high, low = split(mid[...])
    table = last[which * (blocks // 2) : (which + 1) * (blocks // 2), :]
    result = dot(table, jnp.concatenate([high, high], axis=0))
    result += dot(table, jnp.concatenate([low, low], axis=0))
    for i in range(per):
        wide[:, i, :] = result[:, i * width : (i + 1) * width]
    out[...] = wide[...].astype(out.dtype)


def mixer_kernel(seq_size, chan_size, owners, freqs, arrays, *refs):
    sources, weight_hbm, out_ref = refs[:arrays], refs[arrays], refs[arrays + 1]
    held = refs[arrays + 2 : 2 * arrays + 2]
    x_ref, gate_ref, skip_ref, decay_ref, w1_ref, b1_ref, w2_ref, b2_ref, wl_ref = held[:9]
    twiddle, middle, first, last = held[9:]
    (
        pad1,
        pad2,
        hid,
        hidden,
        rows,
        params,
        all_params,
        send_taps,
        recv_taps,
        send_x,
        recv_x,
        lhs,
        taps_spectrum,
        product,
        mid,
        wide,
        send_y,
        recv_y,
        mixed,
        gathered,
        columns,
        send_sems,
        recv_sems,
        local_sems,
    ) = refs[2 * arrays + 2 :]
    block, chans = x_ref.shape
    order = w1_ref.shape[1]
    length = seq_size * block
    half = seq_size // 2
    per = chans // owners
    share = seq_size // chan_size
    feats = out_ref.shape[1]
    d = lax.axis_index("seq")
    c = lax.axis_index("chan")
    base = (half - owners) // 2
    rank = d - base
    is_owner = (rank >= 0) & (rank < owners)
    core = lax.rem(d, 2)
    sibling = d + 1 - 2 * core
    part = chans // 2

    def chan_peer(k):
        return lax.rem(c + k, chan_size)

    def wait_bytes(ref, sem):
        pltpu.make_async_copy(ref, ref, sem).wait()

    def to_seq(source, target, lane, landing, p):
        pltpu.make_async_remote_copy(
            src_ref=source,
            dst_ref=target,
            send_sem=send_sems.at[lane],
            recv_sem=recv_sems.at[landing],
            device_id={"seq": p},
            device_id_type=MESH,
        ).start()

    def to_chan(source, target, lane, p):
        pltpu.make_async_remote_copy(
            src_ref=source,
            dst_ref=target,
            send_sem=send_sems.at[lane],
            recv_sem=recv_sems.at[lane],
            device_id={"chan": p},
            device_id_type=MESH,
        ).start()

    loads = [
        pltpu.make_async_copy(source, target, local_sems.at[i])
        for i, (source, target) in enumerate(zip(sources, held))
    ]
    for load in loads:
        load.start()
    barrier = pltpu.get_barrier_semaphore()

    @pl.when(is_owner)
    def _():
        @pl.loop(1, seq_size)
        def _(k):
            p = lax.rem(d + k, seq_size)
            pl.semaphore_signal(barrier, inc=1, device_id={"seq": p}, device_id_type=MESH)

    @pl.when(jnp.logical_not(is_owner))
    def _():
        pl.semaphore_signal(barrier, inc=1, device_id={"seq": sibling}, device_id_type=MESH)

    @pl.loop(1, chan_size)
    def _(k):
        pl.semaphore_signal(
            barrier, inc=1, device_id={"chan": chan_peer(k)}, device_id_type=MESH
        )

    def weight_part(p):
        return weight_hbm.at[
            pl.ds(pl.multiple_of(core * part, part), part),
            pl.ds(pl.multiple_of(p * feats, feats), feats),
        ]

    own_columns = pltpu.make_async_copy(
        weight_part(c),
        columns.at[c, core],
        local_sems.at[arrays],
    )
    own_columns.start()
    for load in loads:
        load.wait()

    send_x[...] = x_ref[...].astype(F32).T.reshape(owners, per, block).astype(BF16)

    @pl.when(is_owner)
    def _():
        rows[...] = jnp.zeros_like(rows)
        rows[:order, :] = wl_ref[...]
        rows[order : order + 1, :] = decay_ref[...]
        rows[order + 1 : order + 2, :] = skip_ref[...]
        params[...] = rows[...].T.reshape(owners, per, block)
        pl.semaphore_wait(barrier, owners - 1 + chan_size - 1)

    @pl.when(jnp.logical_not(is_owner))
    def _():
        pl.semaphore_wait(barrier, owners + 1 + chan_size - 1)

    @pl.loop(0, owners)
    def _(o):
        @pl.when(o != rank)
        def _():
            to_seq(send_x.at[o], recv_x.at[d], 0, jnp.where(d < half, 0, 1), base + o)

    others = pl.ds(0, (chan_size - 1))

    @pl.when(is_owner)
    def _():
        @pl.loop(1, chan_size)
        def _(k):
            to_chan(params.at[rank], all_params.at[c], 2, chan_peer(k))

        all_params[c] = params[rank]
        recv_x[d] = send_x[rank]
        start = c * (share * block)
        hidden_block(
            start,
            length,
            freqs,
            share * block,
            w1_ref,
            b1_ref,
            w2_ref,
            b2_ref,
            pad1,
            pad2,
            hid,
            hidden,
        )
        wait_bytes(all_params.at[others], recv_sems.at[2])
        taps = filter_taps(
            start, length, order, all_params[...].reshape(chan_size * per, block), hidden[...]
        )
        for q in range(share):
            send_taps[:, q] = taps[:, q * block : (q + 1) * block].reshape(chan_size, per, block)
        here = pl.ds(c * share, share)

        @pl.loop(1, chan_size)
        def _(k):
            p = chan_peer(k)
            to_chan(send_taps.at[p], recv_taps.at[here], 3, p)

        recv_taps[here] = send_taps[c]

    def send_weights():
        @pl.loop(1, chan_size)
        def _(k):
            p = chan_peer(k)
            to_chan(weight_part(p), columns.at[c, core], 4, p)

    def share_weights():
        own_columns.wait()
        wait_bytes(columns.at[others, 0], recv_sems.at[4])
        to_seq(columns.at[:, core], columns.at[:, core], 5, 7, sibling)

    early, late = pl.ds(0, half), pl.ds(half, half)

    @pl.when(is_owner)
    def _():
        wait_bytes(recv_taps.at[pl.ds(0, (chan_size - 1) * share)], recv_sems.at[3])
        stage = taps_stage(first, 0, recv_taps.at[early]) + taps_stage(first, 1, recv_taps.at[late])
        taps_spectrum[...] = spectrum(seq_size, stage, lhs, twiddle, middle)
        wait_bytes(recv_x.at[pl.ds(0, half - 1)], recv_sems.at[0])
        stage = input_stage(first, 0, recv_x.at[early], wide)
        inputs = spectrum(seq_size, stage, lhs, twiddle, middle)
        product[...] = multiply(inputs, taps_spectrum[...])
        inverse(
            seq_size, product[...], 0, mid, twiddle, middle, last, wide, send_y.at[early]
        )

        @pl.loop(1, half)
        def _(k):
            p = lax.rem(d + k, half)
            to_seq(send_y.at[p], recv_y.at[rank], 1, 5, p)

        recv_y[rank] = send_y[d]
        send_weights()
        wait_bytes(recv_y.at[pl.ds(0, owners - 1)], recv_sems.at[5])

    @pl.when(jnp.logical_not(is_owner))
    def _():
        send_weights()
        share_weights()
        wait_bytes(recv_y, recv_sems.at[5])

    convolved = recv_y[...].astype(F32).reshape(chans, block).T
    mixed[...] = (gate_ref[...].astype(F32) * convolved).astype(BF16)
    place = gathered.at[:, pl.ds(pl.multiple_of(c * chans, chans), chans)]

    @pl.loop(1, chan_size)
    def _(k):
        to_chan(mixed, place, 6, chan_peer(k))

    place[...] = mixed[...]

    @pl.when(is_owner)
    def _():
        share_weights()
        wait_bytes(recv_x.at[pl.ds(0, half)], recv_sems.at[1])
        stage = input_stage(first, 1, recv_x.at[late], wide)
        inputs = spectrum(seq_size, stage, lhs, twiddle, middle)
        product[...] += multiply(inputs, taps_spectrum[...])
        inverse(
            seq_size, product[...], 1, mid, twiddle, middle, last, wide, send_y.at[late]
        )

        @pl.loop(0, half)
        def _(k):
            p = half + lax.rem(d + k, half)
            to_seq(send_y.at[p], recv_y.at[rank], 1, 5, p)

    rest = pl.ds(0, (chan_size - 1) * chans)
    wait_bytes(columns.at[:, 0], recv_sems.at[7])
    wait_bytes(gathered.at[:, rest], recv_sems.at[6])
    weights = columns[...].reshape(chan_size * chans, feats)
    out_ref[...] = dot(gathered[...], weights).astype(out_ref.dtype)

    @pl.when(is_owner)
    def _():
        wait_bytes(send_x.at[pl.ds(0, owners - 1)], send_sems.at[0])
        wait_bytes(send_y.at[pl.ds(0, seq_size - 1)], send_sems.at[1])
        wait_bytes(all_params.at[others], send_sems.at[2])
        wait_bytes(send_taps.at[others], send_sems.at[3])

    @pl.when(jnp.logical_not(is_owner))
    def _():
        wait_bytes(send_x, send_sems.at[0])

    wait_bytes(columns.at[others, 0], send_sems.at[4])
    wait_bytes(columns.at[:, 0], send_sems.at[5])
    wait_bytes(gathered.at[:, rest], send_sems.at[6])


def shards(
    mixer_input,
    gate_branch,
    skip_gain,
    decay_rate,
    first_weight,
    first_bias,
    second_weight,
    second_bias,
    last_weight,
    output_weight,
):
    block, chans = mixer_input.shape
    seq_size = lax.axis_size("seq")
    chan_size = lax.axis_size("chan")
    emb, order = first_weight.shape
    feats = output_weight.shape[1] // chan_size
    owners = seq_size // 4
    per = chans // owners
    share = seq_size // chan_size
    length = block * seq_size
    held = [
        mixer_input,
        gate_branch,
        skip_gain.reshape(1, chans),
        decay_rate.reshape(1, chans),
        first_weight,
        first_bias.reshape(1, order),
        second_weight,
        second_bias.reshape(1, order),
        last_weight,
        *[jnp.asarray(table) for table in transform_tables(seq_size, block)],
    ]
    return pl.pallas_call(
        functools.partial(
            mixer_kernel, seq_size, chan_size, owners, band_frequencies(length, emb), len(held)
        ),
        out_shape=jax.ShapeDtypeStruct((block, feats), BF16),
        in_specs=[pl.BlockSpec(memory_space=pltpu.HBM)] * (len(held) + 1),
        out_specs=pl.BlockSpec(memory_space=pltpu.VMEM),
        scratch_shapes=[
            *[pltpu.VMEM(value.shape, value.dtype) for value in held],
            pltpu.VMEM((-(-(emb + 1) // 8) * 8, order), F32),
            pltpu.VMEM((order + 8, order), F32),
            pltpu.VMEM((order + 8, share * block), F32),
            pltpu.VMEM((order, share * block), F32),
            pltpu.VMEM((block, chans), F32),
            pltpu.VMEM((owners, per, block), F32),
            pltpu.VMEM((chan_size, per, block), F32),
            pltpu.VMEM((chan_size, share, per, block), F32),
            pltpu.VMEM((seq_size, per, block), F32),
            pltpu.VMEM((owners, per, block), BF16),
            pltpu.VMEM((seq_size, per, block), BF16),
            pltpu.VMEM((per * seq_size, 2 * block), F32),
            pltpu.VMEM((per * seq_size, 2 * block), F32),
            pltpu.VMEM((per * seq_size, 2 * block), F32),
            pltpu.VMEM((2 * seq_size, per * block), F32),
            pltpu.VMEM((seq_size // 2, per, block), F32),
            pltpu.VMEM((seq_size, per, block), BF16),
            pltpu.VMEM((owners, per, block), BF16),
            pltpu.VMEM((block, chans), BF16),
            pltpu.VMEM((block, chan_size * chans), BF16),
            pltpu.VMEM((chan_size, 2, chans // 2, feats), BF16),
            pltpu.SemaphoreType.DMA((7,)),
            pltpu.SemaphoreType.DMA((8,)),
            pltpu.SemaphoreType.DMA((len(held) + 1,)),
        ],
        compiler_params=pltpu.CompilerParams(
            collective_id=0, has_side_effects=True, vmem_limit_bytes=62 << 20
        ),
    )(*held, output_weight)


def solution(mesh):
    in_specs = (
        P("seq", "chan"),
        P("seq", "chan"),
        P("chan"),
        P("chan"),
        P(),
        P(),
        P(),
        P(),
        P(None, "chan"),
        P("chan", None),
    )
    out_specs = P("seq", "chan")
    return jax.shard_map(shards, mesh=mesh, in_specs=in_specs, out_specs=out_specs, check_vma=False)
```
